512 devices in a mesh: dp: 8 (over x_hi, y), fsdp: 64 (over z, x_lo, core).
Axes of the slice: x: 4 (x_hi: 2, x_lo: 2; x = x_hi * 2 + x_lo), y: 4, z: 16, core: 2. Of those that a mesh axis runs over, the one named last changes fastest.
Arguments:
- samples: bfloat16 [1024, 256, 768], P(('dp', 'fsdp')), may hold values from -6 to 6
- cotangent: bfloat16 [1024, 256, 768], P(('dp', 'fsdp')), may hold values from -6 to 6
- w_in: bfloat16 [3072, 768], P('fsdp'), may hold values from -0.21875 to 0.21875
- w_out: bfloat16 [3072, 768], P('fsdp'), may hold values from -0.21875 to 0.21875
- sketch_in: bfloat16 [768, 16], replicated, may hold values from -0.21875 to 0.21875
- sketch_hidden: bfloat16 [3072, 16], replicated, may hold values from -0.109375 to 0.109375
- targets: float32 [1024], P(('dp', 'fsdp')), may hold values from -6 to 6
Outputs:
- coeffs: float32 [1024], P(('dp', 'fsdp'))
- sketched_step: float32 [512], replicated
The draws below stay inside these ranges and needn't reach their ends.
All inputs are finite; a program needn't handle non-finite values.
Results may differ from the reference program's by a relative error of at most 0.0054.
Values may be sent and summed in bfloat16 or wider, within the bound.
A program may use at most 64 MiB of HBM per device.

```python
import jax
import jax.numpy as jnp
from jax import lax

D = 768
FF = 3072
RANK = 16
POS = 256
SAMP_DEV = 2
FEAT = 512
SAMPLES = 1024


def shard_levels(key, dims, cuts, low, top_value):
    def one(axis_at, blocks):
        draws = jax.random.uniform(jax.random.fold_in(jax.random.fold_in(key, 6), axis_at), (blocks,), jnp.float32, low / len(cuts), top_value / len(cuts))
        return jnp.repeat(jnp.exp(draws), dims[axis_at] // blocks).reshape((-1,) + (1,) * (len(dims) - axis_at - 1))

    factor_of = one(*cuts[0])
    for cut in cuts[1:]:
        factor_of = factor_of * one(*cut)
    return factor_of


def normal_values(key, dims, spread, bound, pieces=(), kind=jnp.bfloat16):
    drawn = jax.random.normal(key, dims, jnp.float32) * spread
    if len(pieces) > 0:
        drawn = shard_levels(key, dims, pieces, -0.22, 0.18) * drawn
    return jnp.clip(drawn, min=-bound, max=bound).astype(kind)


def setup_inputs(seed: int = 0) -> dict:
    key_of = jax.random.split(jax.random.key(seed), 8)
    samples = normal_values(key_of[0], (SAMPLES, POS, D), 1.0, 6.0, ((0, 512),))
    cotangent = normal_values(key_of[1], (SAMPLES, POS, D), 1.0, 6.0, ((0, 512),))
    w_in = normal_values(key_of[2], (FF, D), D ** -0.5, 0.21875, ((0, 64),))
    w_out = normal_values(key_of[3], (FF, D), D ** -0.5, 0.21875, ((0, 64),))
    sketch_in = normal_values(key_of[4], (D, RANK), D ** -0.5, 0.21875)
    sketch_hidden = normal_values(key_of[5], (FF, RANK), FF ** -0.5, 0.109375)
    targets = normal_values(key_of[6], (SAMPLES,), 1.0, 6.0, ((0, 512),), jnp.float32)
    return {"samples": samples, "cotangent": cotangent, "w_in": w_in, "w_out": w_out, "sketch_in": sketch_in, "sketch_hidden": sketch_hidden, "targets": targets}


DAMPING = 0.5

def block_features(x_block, g_block, w_in, w_out, sketch_in, sketch_hidden):
    count, length, width = x_block.shape
    flat_x = x_block.reshape(count * length, width)
    flat_g = g_block.reshape(count * length, width)
    pre = lax.dot_general(flat_x.astype(jnp.float32), w_in.astype(jnp.float32), (((1,), (1,)), ((), ())), preferred_element_type=jnp.float32)
    back = lax.dot_general(flat_g.astype(jnp.float32), w_out.astype(jnp.float32), (((1,), (1,)), ((), ())), preferred_element_type=jnp.float32)
    sig = jax.nn.sigmoid(pre)
    hidden = (pre * sig).astype(jnp.bfloat16)
    slope = (back * sig * (1.0 + pre * (1.0 - sig))).astype(jnp.bfloat16)
    hq = jnp.dot(hidden.astype(jnp.float32), sketch_hidden.astype(jnp.float32), preferred_element_type=jnp.float32)
    dq = jnp.dot(slope.astype(jnp.float32), sketch_hidden.astype(jnp.float32), preferred_element_type=jnp.float32)
    xp = jnp.dot(flat_x.astype(jnp.float32), sketch_in.astype(jnp.float32), preferred_element_type=jnp.float32)
    gp = jnp.dot(flat_g.astype(jnp.float32), sketch_in.astype(jnp.float32), preferred_element_type=jnp.float32)
    first = jnp.einsum('spr,spq->srq', dq.reshape(count, length, -1), xp.reshape(count, length, -1), precision=lax.Precision.HIGHEST) / length
    second = jnp.einsum('spr,spq->srq', hq.reshape(count, length, -1), gp.reshape(count, length, -1), precision=lax.Precision.HIGHEST) / length
    return jnp.concatenate([first.reshape(count, -1), second.reshape(count, -1)], axis=1).astype(jnp.bfloat16)

def reference(samples, cotangent, w_in, w_out, sketch_in, sketch_hidden, targets):
    xs = samples.reshape(-1, SAMP_DEV, POS, D)
    gs = cotangent.reshape(-1, SAMP_DEV, POS, D)
    feats = lax.map(lambda pair: block_features(pair[0], pair[1], w_in, w_out, sketch_in, sketch_hidden), (xs, gs))
    feats = feats.reshape(SAMPLES, FEAT)
    gram = lax.dot_general(feats.astype(jnp.float32), feats.astype(jnp.float32), (((1,), (1,)), ((), ())), preferred_element_type=jnp.float32)
    factor = jnp.linalg.cholesky(gram + DAMPING * jnp.eye(SAMPLES, dtype=jnp.float32))
    coeffs = jax.scipy.linalg.cho_solve((factor, True), targets)
    step = lax.dot_general(feats.astype(jnp.float32), coeffs, (((0,), (0,)), ((), ())), precision=lax.Precision.HIGHEST)
    return (coeffs, step)
```

```python
import jax
import jax.numpy as jnp
from jax import lax
from jax.sharding import PartitionSpec as P

DAMPING = 0.5


def per_device(samples, cotangent, w_in, w_out, sketch_in, sketch_hidden, targets):
    count, length, width = samples.shape
    flat_x = samples.reshape(count * length, width)
    flat_g = cotangent.reshape(count * length, width)
    rows_in = lax.all_gather(w_in, "fsdp", axis=0, tiled=True)
    rows_out = lax.all_gather(w_out, "fsdp", axis=0, tiled=True)
    all_targets = lax.all_gather(targets, ("dp", "fsdp"), axis=0, tiled=True)
    pre = lax.dot_general(
        flat_x, rows_in, (((1,), (1,)), ((), ())), preferred_element_type=jnp.float32
    )
    back = lax.dot_general(
        flat_g, rows_out, (((1,), (1,)), ((), ())), preferred_element_type=jnp.float32
    )
    sig = jax.nn.sigmoid(pre)
    hidden = (pre * sig).astype(jnp.bfloat16)
    slope = (back * sig * (1.0 + pre * (1.0 - sig))).astype(jnp.bfloat16)
    hq = jnp.dot(hidden, sketch_hidden, preferred_element_type=jnp.float32)
    dq = jnp.dot(slope, sketch_hidden, preferred_element_type=jnp.float32)
    xp = jnp.dot(flat_x, sketch_in, preferred_element_type=jnp.float32)
    gp = jnp.dot(flat_g, sketch_in, preferred_element_type=jnp.float32)

    def outer(left, right):
        return (
            jnp.einsum(
                "spr,spq->srq",
                left.reshape(count, length, -1),
                right.reshape(count, length, -1),
                precision=lax.Precision.HIGHEST,
            )
            / length
        ).reshape(count, -1)

    feats = jnp.concatenate([outer(dq, xp), outer(hq, gp)], axis=1).astype(jnp.bfloat16)
    everyone = lax.all_gather(feats, ("dp", "fsdp"), axis=0, tiled=True)
    size = feats.shape[1]
    small = lax.dot_general(
        everyone, everyone, (((0,), (0,)), ((), ())), preferred_element_type=jnp.float32
    )
    right = lax.dot_general(
        everyone.astype(jnp.float32),
        all_targets,
        (((0,), (0,)), ((), ())),
        precision=lax.Precision.HIGHEST,
    )
    factor = jnp.linalg.cholesky(small + DAMPING * jnp.eye(size, dtype=jnp.float32))
    step = jax.scipy.linalg.cho_solve((factor, True), right)
    fitted = jnp.dot(feats.astype(jnp.float32), step, precision=lax.Precision.HIGHEST)
    coeffs = (targets - fitted) / DAMPING
    return (coeffs, step)


def solution(mesh):
    in_specs = (
        P(("dp", "fsdp"), None, None),
        P(("dp", "fsdp"), None, None),
        P("fsdp", None),
        P("fsdp", None),
        P(),
        P(),
        P(("dp", "fsdp")),
    )
    out_specs = (P(("dp", "fsdp")), P())
    return jax.shard_map(
        per_device, mesh=mesh, in_specs=in_specs, out_specs=out_specs, check_vma=False
    )
```

```python
import functools

import jax
import jax.numpy as jnp
from jax import lax
from jax.experimental import pallas as pl
from jax.experimental.pallas import tpu as pltpu
from jax.sharding import PartitionSpec as P

DAMPING = 0.5
NZ, NY, NX = 16, 4, 4
MESH = pl.DeviceIdType.MESH


def position():
    group, member = lax.axis_index("dp"), lax.axis_index("fsdp")
    x = (group // 4) * 2 + (member // 2) % 2
    return x, group % 4, member // 4, member % 2


def device(x, y, z, core):
    return ((x // 2) * 4 + y, z * 4 + (x % 2) * 2 + core)


def greet(partners):
    barrier = pltpu.get_barrier_semaphore()
    for partner in partners:
        pl.semaphore_signal(barrier, inc=1, device_id=partner, device_id_type=MESH)
    pl.semaphore_wait(barrier, len(partners))


def weights_kernel(
    x_ref, g_ref, w_ref, all_ref, px_ref, pg_ref,
    swap_send, swap_recv, local_sem, z_send, z_recv, y_send, y_recv, o_send, o_recv, x_send, x_recv,
):
    x, y, z, core = position()
    low = x % 2
    up, down = (z + 1) % NZ, (z + NZ - 1) % NZ
    y_up, y_down = (y + 1) % NY, (y + NY - 1) % NY
    x_up, x_down = (x + 1) % NX, (x + NX - 1) % NX
    greet([
        device(x, y, up, core), device(x, y, down, core),
        device(x, y_up, z, core), device(x, y_down, z, core),
        device(x_up, y, z, core), device(x_down, y, z, core),
        device(x, y, z, 1 - core),
    ])
    sends = []

    def place(zz, q, lo):
        return all_ref.at[q // 2, zz, lo, q % 2]

    def remote(src, dst, send, recv, target):
        return pltpu.make_async_remote_copy(
            src_ref=src, dst_ref=dst, send_sem=send, recv_sem=recv, device_id=target, device_id_type=MESH
        )

    def start(copy):
        copy.start()
        sends.append(copy)

    def send_x(src, zz, q):
        target = device((x + (q // 2) * 2 + NX - 1) % NX, y, z, core)
        start(remote(src, place(zz, q, low), x_send.at[zz, q], x_recv.at[zz, q], target))

    def send_y(src, zz):
        start(remote(src, place(zz, y, low), y_send.at[0, zz], y_recv.at[0, zz], device(x, y_up, z, core)))
        start(remote(src, place(zz, y, low), y_send.at[1, zz], y_recv.at[1, zz], device(x, y_down, z, core)))

    def wait_recv(dst, recv):
        remote(dst, dst, swap_send.at[0], recv, device(x, y, z, 1 - core)).wait_recv()

    mine = w_ref.at[y // 2, y % 2]
    start(remote(mine, place(z, y, low), z_send.at[0, 1], z_recv.at[0, 1], device(x, y, up, core)))
    start(remote(mine, place(z, y, low), z_send.at[1, 1], z_recv.at[1, 1], device(x, y, down, core)))
    for q in range(4):
        send_x(w_ref.at[q // 2, q % 2], z, q)
    locals_ = []
    for q in range(4):
        copy = pltpu.make_async_copy(w_ref.at[q // 2, q % 2], place(z, q, low), local_sem.at[q])
        copy.start()
        locals_.append(copy)
    start(remote(x_ref, px_ref, swap_send.at[0], swap_recv.at[0], device(x, y, z, 1 - core)))
    start(remote(g_ref, pg_ref, swap_send.at[1], swap_recv.at[1], device(x, y, z, 1 - core)))

    def blocks_of(step):
        found = []
        if 1 <= step <= 8:
            found.append((0, (z + NZ - step) % NZ))
        if 1 <= step <= 7:
            found.append((1, (z + step) % NZ))
        return found

    for step in range(1, 11):
        for way, zz in blocks_of(step):
            here = place(zz, y, low)
            wait_recv(here, z_recv.at[way, step])
            if step < (8 if way == 0 else 7):
                target = device(x, y, up if way == 0 else down, core)
                start(remote(here, here, z_send.at[way, step + 1], z_recv.at[way, step + 1], target))
            send_y(here, zz)
            send_x(here, zz, y)
        for way, zz in blocks_of(step - 1):
            below, above = place(zz, y_down, low), place(zz, y_up, low)
            wait_recv(below, y_recv.at[0, zz])
            wait_recv(above, y_recv.at[1, zz])
            if way == 0:
                start(remote(below, below, o_send.at[zz], o_recv.at[zz], device(x, y_up, z, core)))
            else:
                start(remote(above, above, o_send.at[zz], o_recv.at[zz], device(x, y_down, z, core)))
            send_x(below, zz, y_down)
            send_x(above, zz, y_up)
        for way, zz in blocks_of(step - 2):
            far = (y + 2) % NY
            wait_recv(place(zz, far, low), o_recv.at[zz])
            send_x(place(zz, far, low), zz, far)
    for zz in range(NZ):
        for q in range(4):
            wait_recv(place(zz, q, 1 - low), x_recv.at[zz, q])
    wait_recv(px_ref, swap_recv.at[0])
    wait_recv(pg_ref, swap_recv.at[1])
    for copy in locals_:
        copy.wait()
    for copy in sends:
        copy.wait_send()


def gather_weights(flat_x, flat_g, w_in, w_out):
    rows, width = w_in.shape
    half = rows // 2
    w = jnp.stack([w_in, w_out]).reshape(2, 2, half, width)
    anywhere = pl.BlockSpec(memory_space=pl.ANY)
    sem = pltpu.SemaphoreType.DMA
    return pl.pallas_call(
        weights_kernel,
        out_shape=(
            jax.ShapeDtypeStruct((2, NZ, 2, 2, half, width), w.dtype),
            jax.ShapeDtypeStruct(flat_x.shape, flat_x.dtype),
            jax.ShapeDtypeStruct(flat_g.shape, flat_g.dtype),
        ),
        in_specs=[anywhere] * 3,
        out_specs=(anywhere,) * 3,
        scratch_shapes=[
            sem((2,)), sem((2,)), sem((4,)), sem((2, 9)), sem((2, 9)), sem((2, NZ)), sem((2, NZ)),
            sem((NZ,)), sem((NZ,)), sem((NZ, 4)), sem((NZ, 4)),
        ],
        compiler_params=pltpu.CompilerParams(collective_id=0, has_side_effects=True),
        name="gather_weights",
    )(flat_x, flat_g, w)


def features_kernel(
    own_ref, other_ref, targets_ref, f_ref, got, zbuf, wide,
    swap_send, swap_recv, a_send, a_recv, b_send, b_recv, y_send, y_recv, x_send, x_recv, c_send, c_recv,
):
    x, y, z, core = position()
    high, low = z // 4, z % 4
    near = [device(x, y, high * 4 + (low + d) % 4, core) for d in range(1, 4)]
    far = [device(x, y, ((high + d) % 4) * 4 + low, core) for d in range(1, 4)]
    along_y = [device(x, (y + d) % NY, z, core) for d in range(1, 4)]
    along_x = [device((x + d) % NX, y, z, core) for d in range(1, 4)]
    partner = device(x, y, z, 1 - core)
    greet(near + far + along_y + along_x + [partner])

    def remote(src, dst, send, recv, target):
        return pltpu.make_async_remote_copy(
            src_ref=src, dst_ref=dst, send_sem=send, recv_sem=recv, device_id=target, device_id_type=MESH
        )

    def exchange(mine, theirs, send, recv, partners):
        copies = []
        for d, target in enumerate(partners):
            copy = remote(mine, mine, send.at[d], recv.at[d], target)
            copy.start()
            copies.append(copy)
        for d in range(len(partners)):
            remote(theirs[d], theirs[d], send.at[d], recv.at[d], partners[d]).wait_recv()
        return copies

    swap = remote(other_ref, got, swap_send, swap_recv, partner)
    swap.start()
    swap.wait_recv()
    feats = own_ref[...] + got[...]
    t = targets_ref[...]
    high_t = t.astype(jnp.bfloat16).astype(jnp.float32)
    mid_t = (t - high_t).astype(jnp.bfloat16).astype(jnp.float32)
    low_t = t - high_t - mid_t
    lane = lax.broadcasted_iota(jnp.int32, (2, 128), 1)
    tail = jnp.where(lane == 0, high_t, jnp.where(lane == 1, mid_t, jnp.where(lane == 2, low_t, 0.0)))
    size = feats.shape[1]
    zbuf[z, :, 0:size] = feats.astype(jnp.bfloat16)
    zbuf[z, :, size:] = tail.astype(jnp.bfloat16)
    sends = [swap]
    sends += exchange(
        zbuf.at[z], [zbuf.at[high * 4 + (low + 4 - d) % 4] for d in range(1, 4)], a_send, a_recv, near
    )
    sends += exchange(
        zbuf.at[pl.ds(high * 4, 4)],
        [zbuf.at[pl.ds(((high + 4 - d) % 4) * 4, 4)] for d in range(1, 4)],
        b_send, b_recv, far,
    )
    for zz in range(NZ):
        wide[2 * zz:2 * zz + 2, :] = zbuf[zz].astype(jnp.float32)
    base = core * 16 + x * 4
    f_ref[base + y] = wide[...].astype(jnp.bfloat16)
    sends += exchange(
        f_ref.at[base + y], [f_ref.at[base + (y + 4 - d) % NY] for d in range(1, 4)], y_send, y_recv, along_y
    )
    sends += exchange(
        f_ref.at[pl.ds(base, 4)],
        [f_ref.at[pl.ds(core * 16 + ((x + 4 - d) % NX) * 4, 4)] for d in range(1, 4)],
        x_send, x_recv, along_x,
    )
    sends += exchange(
        f_ref.at[pl.ds(core * 16, 16)], [f_ref.at[pl.ds((1 - core) * 16, 16)]], c_send, c_recv, [partner]
    )
    for copy in sends:
        copy.wait_send()


def gather_features(own, other, targets):
    size = own.shape[1]
    inside = pl.BlockSpec(memory_space=pltpu.VMEM)
    sem = pltpu.SemaphoreType.DMA
    return pl.pallas_call(
        features_kernel,
        out_shape=jax.ShapeDtypeStruct((32, 32, size + 128), jnp.bfloat16),
        in_specs=[inside] * 3,
        out_specs=inside,
        scratch_shapes=[
            pltpu.VMEM((2, size), jnp.float32),
            pltpu.VMEM((NZ, 2, size + 128), jnp.bfloat16),
            pltpu.VMEM((32, size + 128), jnp.float32),
            sem, sem, sem((3,)), sem((3,)), sem((3,)), sem((3,)), sem((3,)), sem((3,)),
            sem((3,)), sem((3,)), sem((1,)), sem((1,)),
        ],
        compiler_params=pltpu.CompilerParams(collective_id=1, has_side_effects=True),
        name="gather_features",
    )(own, other, targets)


def partial_features(flat_x, flat_g, rows_in, rows_out, sketch_in, sketch_rows, count):
    pre = lax.dot_general(flat_x, rows_in, (((1,), (1,)), ((), ())), preferred_element_type=jnp.float32)
    back = lax.dot_general(flat_g, rows_out, (((1,), (1,)), ((), ())), preferred_element_type=jnp.float32)
    sig = jax.nn.sigmoid(pre)
    hidden = (pre * sig).astype(jnp.bfloat16)
    slope = (back * sig * (1.0 + pre * (1.0 - sig))).astype(jnp.bfloat16)
    hq = jnp.dot(hidden, sketch_rows, preferred_element_type=jnp.float32)
    dq = jnp.dot(slope, sketch_rows, preferred_element_type=jnp.float32)
    xp = jnp.dot(flat_x, sketch_in, preferred_element_type=jnp.float32)
    gp = jnp.dot(flat_g, sketch_in, preferred_element_type=jnp.float32)
    length = flat_x.shape[0] // count

    def outer(left, right):
        return (
            jnp.einsum(
                "spr,spq->srq",
                left.reshape(count, length, -1),
                right.reshape(count, length, -1),
                precision=lax.Precision.HIGHEST,
            )
            / length
        ).reshape(count, -1)

    return jnp.concatenate([outer(dq, xp), outer(hq, gp)], axis=1)


def per_device(samples, cotangent, w_in, w_out, sketch_in, sketch_hidden, targets):
    count, length, width = samples.shape
    flat_x = samples.reshape(count * length, width)
    flat_g = cotangent.reshape(count * length, width)
    rows = w_in.shape[0]
    weights, other_x, other_g = gather_weights(flat_x, flat_g, w_in, w_out)
    rows_in, rows_out = weights[0].reshape(-1, width), weights[1].reshape(-1, width)
    core = lax.axis_index("fsdp") % 2
    sketch_rows = lax.dynamic_index_in_dim(
        sketch_hidden.reshape(NZ * 2, 2, rows, -1), core, 1, keepdims=False
    ).reshape(NZ * 2 * rows, -1)
    own = partial_features(flat_x, flat_g, rows_in, rows_out, sketch_in, sketch_rows, count)
    other = partial_features(other_x, other_g, rows_in, rows_out, sketch_in, sketch_rows, count)
    table = gather_features(own, other, targets.reshape(count, 1))
    size = own.shape[1]
    table = table.reshape(-1, size + 128)
    everyone = table[:, :size]
    pieces = table[:, size:].astype(jnp.float32)
    all_targets = pieces[:, 0] + pieces[:, 1] + pieces[:, 2]
    small = lax.dot_general(
        everyone, everyone, (((0,), (0,)), ((), ())), preferred_element_type=jnp.float32
    )
    right = lax.dot_general(
        everyone.astype(jnp.float32),
        all_targets,
        (((0,), (0,)), ((), ())),
        precision=lax.Precision.HIGHEST,
    )
    factor = jnp.linalg.cholesky(small + DAMPING * jnp.eye(size, dtype=jnp.float32))
    step = jax.scipy.linalg.cho_solve((factor, True), right)
    x, y, z, core = position()
    start = (core * 16 + x * 4 + y) * 32 + z * count
    feats = lax.dynamic_slice_in_dim(everyone, start, count, 0)
    fitted = jnp.dot(feats.astype(jnp.float32), step, precision=lax.Precision.HIGHEST)
    coeffs = (targets - fitted) / DAMPING
    return (coeffs, step)


def solution(mesh):
    in_specs = (
        P(("dp", "fsdp"), None, None),
        P(("dp", "fsdp"), None, None),
        P("fsdp", None),
        P("fsdp", None),
        P(),
        P(),
        P(("dp", "fsdp")),
    )
    out_specs = (P(("dp", "fsdp")), P())
    return jax.shard_map(
        per_device, mesh=mesh, in_specs=in_specs, out_specs=out_specs, check_vma=False
    )
```

```python
import jax
import jax.numpy as jnp
from jax import lax
from jax.experimental import pallas as pl
from jax.experimental.pallas import tpu as pltpu
from jax.sharding import PartitionSpec as P

DAMPING = 0.5
NZ, NY, NX = 16, 4, 4
MESH = pl.DeviceIdType.MESH


def position():
    group, member = lax.axis_index("dp"), lax.axis_index("fsdp")
    x = (group // 4) * 2 + (member // 2) % 2
    return x, group % 4, member // 4, member % 2


def device(x, y, z, core):
    return ((x // 2) * 4 + y, z * 4 + (x % 2) * 2 + core)


def greet(partners):
    barrier = pltpu.get_barrier_semaphore()
    for partner in partners:
        pl.semaphore_signal(barrier, inc=1, device_id=partner, device_id_type=MESH)
    pl.semaphore_wait(barrier, len(partners))


def weights_kernel(
    x_ref, g_ref, w_ref, all_ref, px_ref, pg_ref,
    swap_send, swap_recv, local_sem, z_send, z_recv, y_send, y_recv, o_send, o_recv, x_send, x_recv,
):
    x, y, z, core = position()
    low = x % 2
    up, down = (z + 1) % NZ, (z + NZ - 1) % NZ
    y_up, y_down = (y + 1) % NY, (y + NY - 1) % NY
    x_up, x_down = (x + 1) % NX, (x + NX - 1) % NX
    greet([
        device(x, y, up, core), device(x, y, down, core),
        device(x, y_up, z, core), device(x, y_down, z, core),
        device(x_up, y, z, core), device(x_down, y, z, core),
        device(x, y, z, 1 - core),
    ])
    sends = []

    def place(zz, q, lo):
        return all_ref.at[q // 2, zz, lo, q % 2]

    def remote(src, dst, send, recv, target):
        return pltpu.make_async_remote_copy(
            src_ref=src, dst_ref=dst, send_sem=send, recv_sem=recv, device_id=target, device_id_type=MESH
        )

    def start(copy):
        copy.start()
        sends.append(copy)

    def send_x(src, zz, q):
        target = device((x + (q // 2) * 2 + NX - 1) % NX, y, z, core)
        start(remote(src, place(zz, q, low), x_send.at[zz, q], x_recv.at[zz, q], target))

    def send_y(src, zz):
        start(remote(src, place(zz, y, low), y_send.at[0, zz], y_recv.at[0, zz], device(x, y_up, z, core)))
        start(remote(src, place(zz, y, low), y_send.at[1, zz], y_recv.at[1, zz], device(x, y_down, z, core)))

    def wait_recv(dst, recv):
        remote(dst, dst, swap_send.at[0], recv, device(x, y, z, 1 - core)).wait_recv()

    mine = w_ref.at[y // 2, y % 2]
    start(remote(mine, place(z, y, low), z_send.at[0, 1], z_recv.at[0, 1], device(x, y, up, core)))
    start(remote(mine, place(z, y, low), z_send.at[1, 1], z_recv.at[1, 1], device(x, y, down, core)))
    for q in range(4):
        send_x(w_ref.at[q // 2, q % 2], z, q)
    locals_ = []
    for q in range(4):
        copy = pltpu.make_async_copy(w_ref.at[q // 2, q % 2], place(z, q, low), local_sem.at[q])
        copy.start()
        locals_.append(copy)
    start(remote(x_ref, px_ref, swap_send.at[0], swap_recv.at[0], device(x, y, z, 1 - core)))
    start(remote(g_ref, pg_ref, swap_send.at[1], swap_recv.at[1], device(x, y, z, 1 - core)))

    def blocks_of(step):
        found = []
        if 1 <= step <= 8:
            found.append((0, (z + NZ - step) % NZ))
        if 1 <= step <= 7:
            found.append((1, (z + step) % NZ))
        return found

    for step in range(1, 11):
        for way, zz in blocks_of(step):
            here = place(zz, y, low)
            wait_recv(here, z_recv.at[way, step])
            if step < (8 if way == 0 else 7):
                target = device(x, y, up if way == 0 else down, core)
                start(remote(here, here, z_send.at[way, step + 1], z_recv.at[way, step + 1], target))
            send_y(here, zz)
            send_x(here, zz, y)
        for way, zz in blocks_of(step - 1):
            below, above = place(zz, y_down, low), place(zz, y_up, low)
            wait_recv(below, y_recv.at[0, zz])
            wait_recv(above, y_recv.at[1, zz])
            if way == 0:
                start(remote(below, below, o_send.at[zz], o_recv.at[zz], device(x, y_up, z, core)))
            else:
                start(remote(above, above, o_send.at[zz], o_recv.at[zz], device(x, y_down, z, core)))
            send_x(below, zz, y_down)
            send_x(above, zz, y_up)
        for way, zz in blocks_of(step - 2):
            far = (y + 2) % NY
            wait_recv(place(zz, far, low), o_recv.at[zz])
            send_x(place(zz, far, low), zz, far)
    for zz in range(NZ):
        for q in range(4):
            wait_recv(place(zz, q, 1 - low), x_recv.at[zz, q])
    wait_recv(px_ref, swap_recv.at[0])
    wait_recv(pg_ref, swap_recv.at[1])
    for copy in locals_:
        copy.wait()
    for copy in sends:
        copy.wait_send()


def gather_weights(flat_x, flat_g, w_in, w_out):
    rows, width = w_in.shape
    half = rows // 2
    w = jnp.stack([w_in, w_out]).reshape(2, 2, half, width)
    anywhere = pl.BlockSpec(memory_space=pl.ANY)
    sem = pltpu.SemaphoreType.DMA
    return pl.pallas_call(
        weights_kernel,
        out_shape=(
            jax.ShapeDtypeStruct((2, NZ, 2, 2, half, width), w.dtype),
            jax.ShapeDtypeStruct(flat_x.shape, flat_x.dtype),
            jax.ShapeDtypeStruct(flat_g.shape, flat_g.dtype),
        ),
        in_specs=[anywhere] * 3,
        out_specs=(anywhere,) * 3,
        scratch_shapes=[
            sem((2,)), sem((2,)), sem((4,)), sem((2, 9)), sem((2, 9)), sem((2, NZ)), sem((2, NZ)),
            sem((NZ,)), sem((NZ,)), sem((NZ, 4)), sem((NZ, 4)),
        ],
        compiler_params=pltpu.CompilerParams(collective_id=0, has_side_effects=True),
        name="gather_weights",
    )(flat_x, flat_g, w)


def features_kernel(
    own_ref, other_ref, targets_ref, f_ref, got, zbuf, wide,
    swap_send, swap_recv, a_send, a_recv, b_send, b_recv, y_send, y_recv, x_send, x_recv, c_send, c_recv,
):
    x, y, z, core = position()
    high, low = z // 4, z % 4
    near = [device(x, y, high * 4 + (low + d) % 4, core) for d in range(1, 4)]
    far = [device(x, y, ((high + d) % 4) * 4 + low, core) for d in range(1, 4)]
    along_y = [device(x, (y + d) % NY, z, core) for d in range(1, 4)]
    along_x = [device((x + d) % NX, y, z, core) for d in range(1, 4)]
    partner = device(x, y, z, 1 - core)
    greet(near + far + along_y + along_x + [partner])

    def remote(src, dst, send, recv, target):
        return pltpu.make_async_remote_copy(
            src_ref=src, dst_ref=dst, send_sem=send, recv_sem=recv, device_id=target, device_id_type=MESH
        )

    def exchange(mine, theirs, send, recv, partners):
        copies = []
        for d, target in enumerate(partners):
            copy = remote(mine, mine, send.at[d], recv.at[d], target)
            copy.start()
            copies.append(copy)
        for d in range(len(partners)):
            remote(theirs[d], theirs[d], send.at[d], recv.at[d], partners[d]).wait_recv()
        return copies

    swap = remote(other_ref, got, swap_send, swap_recv, partner)
    swap.start()
    swap.wait_recv()
    feats = own_ref[...] + got[...]
    t = targets_ref[...]
    high_t = t.astype(jnp.bfloat16).astype(jnp.float32)
    mid_t = (t - high_t).astype(jnp.bfloat16).astype(jnp.float32)
    low_t = t - high_t - mid_t
    lane = lax.broadcasted_iota(jnp.int32, (2, 128), 1)
    tail = jnp.where(lane == 0, high_t, jnp.where(lane == 1, mid_t, jnp.where(lane == 2, low_t, 0.0)))
    size = feats.shape[1]
    zbuf[z, :, 0:size] = feats.astype(jnp.bfloat16)
    zbuf[z, :, size:] = tail.astype(jnp.bfloat16)
    sends = [swap]
    sends += exchange(
        zbuf.at[z], [zbuf.at[high * 4 + (low + 4 - d) % 4] for d in range(1, 4)], a_send, a_recv, near
    )
    sends += exchange(
        zbuf.at[pl.ds(high * 4, 4)],
        [zbuf.at[pl.ds(((high + 4 - d) % 4) * 4, 4)] for d in range(1, 4)],
        b_send, b_recv, far,
    )
    for zz in range(NZ):
        wide[2 * zz:2 * zz + 2, :] = zbuf[zz].astype(jnp.float32)
    base = core * 16 + x * 4
    f_ref[base + y] = wide[...].astype(jnp.bfloat16)
    sends += exchange(
        f_ref.at[base + y], [f_ref.at[base + (y + 4 - d) % NY] for d in range(1, 4)], y_send, y_recv, along_y
    )
    sends += exchange(
        f_ref.at[pl.ds(base, 4)],
        [f_ref.at[pl.ds(core * 16 + ((x + 4 - d) % NX) * 4, 4)] for d in range(1, 4)],
        x_send, x_recv, along_x,
    )
    sends += exchange(
        f_ref.at[pl.ds(core * 16, 16)], [f_ref.at[pl.ds((1 - core) * 16, 16)]], c_send, c_recv, [partner]
    )
    for copy in sends:
        copy.wait_send()


def gather_features(own, other, targets):
    size = own.shape[1]
    inside = pl.BlockSpec(memory_space=pltpu.VMEM)
    sem = pltpu.SemaphoreType.DMA
    return pl.pallas_call(
        features_kernel,
        out_shape=jax.ShapeDtypeStruct((32, 32, size + 128), jnp.bfloat16),
        in_specs=[inside] * 3,
        out_specs=inside,
        scratch_shapes=[
            pltpu.VMEM((2, size), jnp.float32),
            pltpu.VMEM((NZ, 2, size + 128), jnp.bfloat16),
            pltpu.VMEM((32, size + 128), jnp.float32),
            sem, sem, sem((3,)), sem((3,)), sem((3,)), sem((3,)), sem((3,)), sem((3,)),
            sem((3,)), sem((3,)), sem((1,)), sem((1,)),
        ],
        compiler_params=pltpu.CompilerParams(collective_id=1, has_side_effects=True),
        name="gather_features",
    )(own, other, targets)


def invert(m):
    side = m.shape[0]
    lane = lax.broadcasted_iota(jnp.int32, m.shape, 1)
    sub = lax.broadcasted_iota(jnp.int32, m.shape, 0)
    for k in range(0, side, 2):
        j = k + 1
        c0 = jnp.broadcast_to(m[:, k:k + 1], m.shape)
        c1 = jnp.broadcast_to(m[:, j:j + 1], m.shape)
        inv0 = 1.0 / c0[k:k + 1, :]
        r0 = jnp.where(lane[0:1] == k, 1.0, m[k:k + 1, :]) * inv0
        r1 = jnp.where(lane[0:1] == k, 0.0, m[j:j + 1, :]) - c0[j:j + 1, :] * r0
        across = c1[k:k + 1, :] * inv0
        inv1 = 1.0 / (c1[j:j + 1, :] - c0[j:j + 1, :] * across)
        r1 = jnp.where(lane[0:1] == j, 1.0, r1) * inv1
        c0 = jnp.where(sub == k, -1.0, c0)
        c1 = jnp.where(sub == k, 0.0, c1) - c0 * across
        c1 = jnp.where(sub == j, -1.0, c1)
        m = jnp.where((lane == k) | (sub == k), 0.0, m) - c0 * r0
        m = jnp.where((lane == j) | (sub == j), 0.0, m) - c1 * r1
    return m


def solve_kernel(a_ref, out_ref, work):
    size = a_ref.shape[0]
    side = 128
    high = lax.Precision.HIGHEST
    diagonal = lax.broadcasted_iota(jnp.int32, a_ref.shape, 0) == lax.broadcasted_iota(jnp.int32, a_ref.shape, 1)
    work[...] = a_ref[...] + jnp.where(diagonal, DAMPING, 0.0)

    def body(block, carry):
        here = pl.ds(pl.multiple_of(block * side, side), side)
        rows = jnp.dot(invert(work[here, here]), work[here, :], precision=high, preferred_element_type=jnp.float32)
        work[...] = work[...] - jnp.dot(work[:, here], rows, precision=high, preferred_element_type=jnp.float32)
        work[here, :] = rows
        return carry

    lax.fori_loop(0, size // side, body, 0)
    out_ref[...] = lax.dot_general(
        jnp.ones((8, a_ref.shape[1] - size), jnp.float32),
        work[:, size:],
        (((1,), (1,)), ((), ())),
        precision=high,
        preferred_element_type=jnp.float32,
    )


def solve(extended):
    return pl.pallas_call(
        solve_kernel,
        out_shape=jax.ShapeDtypeStruct((8, extended.shape[0]), jnp.float32),
        in_specs=[pl.BlockSpec(memory_space=pltpu.VMEM)],
        out_specs=pl.BlockSpec(memory_space=pltpu.VMEM),
        scratch_shapes=[pltpu.VMEM(extended.shape, jnp.float32)],
        name="solve",
    )(extended)[0]


def partial_features(flat_x, flat_g, rows_in, rows_out, sketch_in, sketch_rows, count):
    pre = lax.dot_general(flat_x, rows_in, (((1,), (1,)), ((), ())), preferred_element_type=jnp.float32)
    back = lax.dot_general(flat_g, rows_out, (((1,), (1,)), ((), ())), preferred_element_type=jnp.float32)
    sig = jax.nn.sigmoid(pre)
    hidden = (pre * sig).astype(jnp.bfloat16)
    slope = (back * sig * (1.0 + pre * (1.0 - sig))).astype(jnp.bfloat16)
    hq = jnp.dot(hidden, sketch_rows, preferred_element_type=jnp.float32)
    dq = jnp.dot(slope, sketch_rows, preferred_element_type=jnp.float32)
    xp = jnp.dot(flat_x, sketch_in, preferred_element_type=jnp.float32)
    gp = jnp.dot(flat_g, sketch_in, preferred_element_type=jnp.float32)
    length = flat_x.shape[0] // count

    def outer(left, right):
        return (
            jnp.einsum(
                "spr,spq->srq",
                left.reshape(count, length, -1),
                right.reshape(count, length, -1),
                precision=lax.Precision.HIGHEST,
            )
            / length
        ).reshape(count, -1)

    return jnp.concatenate([outer(dq, xp), outer(hq, gp)], axis=1)


def per_device(samples, cotangent, w_in, w_out, sketch_in, sketch_hidden, targets):
    count, length, width = samples.shape
    flat_x = samples.reshape(count * length, width)
    flat_g = cotangent.reshape(count * length, width)
    rows = w_in.shape[0]
    weights, other_x, other_g = gather_weights(flat_x, flat_g, w_in, w_out)
    rows_in, rows_out = weights[0].reshape(-1, width), weights[1].reshape(-1, width)
    core = lax.axis_index("fsdp") % 2
    sketch_rows = lax.dynamic_index_in_dim(
        sketch_hidden.reshape(NZ * 2, 2, rows, -1), core, 1, keepdims=False
    ).reshape(NZ * 2 * rows, -1)
    own = partial_features(flat_x, flat_g, rows_in, rows_out, sketch_in, sketch_rows, count)
    other = partial_features(other_x, other_g, rows_in, rows_out, sketch_in, sketch_rows, count)
    table = gather_features(own, other, targets.reshape(count, 1))
    size = own.shape[1]
    table = table.reshape(-1, size + 128)
    everyone = table[:, :size]
    extended = lax.dot_general(
        everyone, table, (((0,), (0,)), ((), ())), preferred_element_type=jnp.float32
    )
    step = solve(extended)
    x, y, z, core = position()
    start = (core * 16 + x * 4 + y) * 32 + z * count
    feats = lax.dynamic_slice_in_dim(everyone, start, count, 0)
    fitted = jnp.dot(feats.astype(jnp.float32), step, precision=lax.Precision.HIGHEST)
    coeffs = (targets - fitted) / DAMPING
    return (coeffs, step)


def solution(mesh):
    in_specs = (
        P(("dp", "fsdp"), None, None),
        P(("dp", "fsdp"), None, None),
        P("fsdp", None),
        P("fsdp", None),
        P(),
        P(),
        P(("dp", "fsdp")),
    )
    out_specs = (P(("dp", "fsdp")), P())
    return jax.shard_map(
        per_device, mesh=mesh, in_specs=in_specs, out_specs=out_specs, check_vma=False
    )
```

```python
import jax
import jax.numpy as jnp
from jax import lax
from jax.experimental import pallas as pl
from jax.experimental.pallas import tpu as pltpu
from jax.sharding import PartitionSpec as P

DAMPING = 0.5
NZ, NY, NX = 16, 4, 4
MESH = pl.DeviceIdType.MESH


def position():
    group, member = lax.axis_index("dp"), lax.axis_index("fsdp")
    x = (group // 4) * 2 + (member // 2) % 2
    return x, group % 4, member // 4, member % 2


def device(x, y, z, core):
    return ((x // 2) * 4 + y, z * 4 + (x % 2) * 2 + core)


def greet(partners):
    barrier = pltpu.get_barrier_semaphore()
    for partner in partners:
        pl.semaphore_signal(barrier, inc=1, device_id=partner, device_id_type=MESH)
    pl.semaphore_wait(barrier, len(partners))


def weights_kernel(
    x_ref, g_ref, w_ref, all_ref, px_ref, pg_ref,
    swap_send, swap_recv, local_sem, z_send, z_recv, y_send, y_recv, o_send, o_recv, x_send, x_recv,
):
    x, y, z, core = position()
    low = x % 2
    up, down = (z + 1) % NZ, (z + NZ - 1) % NZ
    y_up, y_down = (y + 1) % NY, (y + NY - 1) % NY
    x_up, x_down = (x + 1) % NX, (x + NX - 1) % NX
    greet([
        device(x, y, up, core), device(x, y, down, core),
        device(x, y_up, z, core), device(x, y_down, z, core),
        device(x_up, y, z, core), device(x_down, y, z, core),
        device(x, y, z, 1 - core),
    ])
    sends = []

    def place(zz, q, lo):
        return all_ref.at[q // 2, zz, lo, q % 2]

    def remote(src, dst, send, recv, target):
        return pltpu.make_async_remote_copy(
            src_ref=src, dst_ref=dst, send_sem=send, recv_sem=recv, device_id=target, device_id_type=MESH
        )

    def start(copy):
        copy.start()
        sends.append(copy)

    def send_x(src, zz, q):
        target = device((x + (q // 2) * 2 + NX - 1) % NX, y, z, core)
        start(remote(src, place(zz, q, low), x_send.at[zz, q], x_recv.at[zz, q], target))

    def send_y(src, zz):
        start(remote(src, place(zz, y, low), y_send.at[0, zz], y_recv.at[0, zz], device(x, y_up, z, core)))
        start(remote(src, place(zz, y, low), y_send.at[1, zz], y_recv.at[1, zz], device(x, y_down, z, core)))

    def wait_recv(dst, recv):
        remote(dst, dst, swap_send.at[0], recv, device(x, y, z, 1 - core)).wait_recv()

    mine = w_ref.at[y // 2, y % 2]
    start(remote(mine, place(z, y, low), z_send.at[0, 1], z_recv.at[0, 1], device(x, y, up, core)))
    start(remote(mine, place(z, y, low), z_send.at[1, 1], z_recv.at[1, 1], device(x, y, down, core)))
    for q in range(4):
        send_x(w_ref.at[q // 2, q % 2], z, q)
    locals_ = []
    for q in range(4):
        copy = pltpu.make_async_copy(w_ref.at[q // 2, q % 2], place(z, q, low), local_sem.at[q])
        copy.start()
        locals_.append(copy)
    start(remote(x_ref, px_ref, swap_send.at[0], swap_recv.at[0], device(x, y, z, 1 - core)))
    start(remote(g_ref, pg_ref, swap_send.at[1], swap_recv.at[1], device(x, y, z, 1 - core)))

    def blocks_of(step):
        found = []
        if 1 <= step <= 8:
            found.append((0, (z + NZ - step) % NZ))
        if 1 <= step <= 7:
            found.append((1, (z + step) % NZ))
        return found

    for step in range(1, 11):
        for way, zz in blocks_of(step):
            here = place(zz, y, low)
            wait_recv(here, z_recv.at[way, step])
            if step < (8 if way == 0 else 7):
                target = device(x, y, up if way == 0 else down, core)
                start(remote(here, here, z_send.at[way, step + 1], z_recv.at[way, step + 1], target))
            send_y(here, zz)
            send_x(here, zz, y)
        for way, zz in blocks_of(step - 1):
            below, above = place(zz, y_down, low), place(zz, y_up, low)
            wait_recv(below, y_recv.at[0, zz])
            wait_recv(above, y_recv.at[1, zz])
            if way == 0:
                start(remote(below, below, o_send.at[zz], o_recv.at[zz], device(x, y_up, z, core)))
            else:
                start(remote(above, above, o_send.at[zz], o_recv.at[zz], device(x, y_down, z, core)))
            send_x(below, zz, y_down)
            send_x(above, zz, y_up)
        for way, zz in blocks_of(step - 2):
            far = (y + 2) % NY
            wait_recv(place(zz, far, low), o_recv.at[zz])
            send_x(place(zz, far, low), zz, far)
    for zz in range(NZ):
        for q in range(4):
            wait_recv(place(zz, q, 1 - low), x_recv.at[zz, q])
    wait_recv(px_ref, swap_recv.at[0])
    wait_recv(pg_ref, swap_recv.at[1])
    for copy in locals_:
        copy.wait()
    for copy in sends:
        copy.wait_send()


def gather_weights(flat_x, flat_g, w_in, w_out):
    rows, width = w_in.shape
    half = rows // 2
    w = jnp.stack([w_in, w_out]).reshape(2, 2, half, width)
    anywhere = pl.BlockSpec(memory_space=pl.ANY)
    sem = pltpu.SemaphoreType.DMA
    return pl.pallas_call(
        weights_kernel,
        out_shape=(
            jax.ShapeDtypeStruct((2, NZ, 2, 2, half, width), w.dtype),
            jax.ShapeDtypeStruct(flat_x.shape, flat_x.dtype),
            jax.ShapeDtypeStruct(flat_g.shape, flat_g.dtype),
        ),
        in_specs=[anywhere] * 3,
        out_specs=(anywhere,) * 3,
        scratch_shapes=[
            sem((2,)), sem((2,)), sem((4,)), sem((2, 9)), sem((2, 9)), sem((2, NZ)), sem((2, NZ)),
            sem((NZ,)), sem((NZ,)), sem((NZ, 4)), sem((NZ, 4)),
        ],
        compiler_params=pltpu.CompilerParams(collective_id=0, has_side_effects=True),
        name="gather_weights",
    )(flat_x, flat_g, w)


def features_kernel(
    own_ref, other_ref, targets_ref, f_ref, got, zbuf, wide,
    swap_send, swap_recv, a_send, a_recv, b_send, b_recv, y_send, y_recv, x_send, x_recv, c_send, c_recv,
):
    x, y, z, core = position()
    high, low = z // 4, z % 4
    near = [device(x, y, high * 4 + (low + d) % 4, core) for d in range(1, 4)]
    far = [device(x, y, ((high + d) % 4) * 4 + low, core) for d in range(1, 4)]
    along_y = [device(x, (y + d) % NY, z, core) for d in range(1, 4)]
    along_x = [device((x + d) % NX, y, z, core) for d in range(1, 4)]
    partner = device(x, y, z, 1 - core)
    greet(near + far + along_y + along_x + [partner])

    def remote(src, dst, send, recv, target):
        return pltpu.make_async_remote_copy(
            src_ref=src, dst_ref=dst, send_sem=send, recv_sem=recv, device_id=target, device_id_type=MESH
        )

    def exchange(mine, theirs, send, recv, partners):
        copies = []
        for d, target in enumerate(partners):
            copy = remote(mine, mine, send.at[d], recv.at[d], target)
            copy.start()
            copies.append(copy)
        for d in range(len(partners)):
            remote(theirs[d], theirs[d], send.at[d], recv.at[d], partners[d]).wait_recv()
        return copies

    swap = remote(other_ref, got, swap_send, swap_recv, partner)
    swap.start()
    swap.wait_recv()
    feats = own_ref[...] + got[...]
    t = targets_ref[...]
    high_t = t.astype(jnp.bfloat16).astype(jnp.float32)
    mid_t = (t - high_t).astype(jnp.bfloat16).astype(jnp.float32)
    low_t = t - high_t - mid_t
    lane = lax.broadcasted_iota(jnp.int32, (2, 128), 1)
    tail = jnp.where(lane == 0, high_t, jnp.where(lane == 1, mid_t, jnp.where(lane == 2, low_t, 0.0)))
    size = feats.shape[1]
    zbuf[z, :, 0:size] = feats.astype(jnp.bfloat16)
    zbuf[z, :, size:] = tail.astype(jnp.bfloat16)
    sends = [swap]
    sends += exchange(
        zbuf.at[z], [zbuf.at[high * 4 + (low + 4 - d) % 4] for d in range(1, 4)], a_send, a_recv, near
    )
    sends += exchange(
        zbuf.at[pl.ds(high * 4, 4)],
        [zbuf.at[pl.ds(((high + 4 - d) % 4) * 4, 4)] for d in range(1, 4)],
        b_send, b_recv, far,
    )
    for zz in range(NZ):
        wide[2 * zz:2 * zz + 2, :] = zbuf[zz].astype(jnp.float32)
    base = core * 16 + x * 4
    f_ref[base + y] = wide[...].astype(jnp.bfloat16)
    sends += exchange(
        f_ref.at[base + y], [f_ref.at[base + (y + 4 - d) % NY] for d in range(1, 4)], y_send, y_recv, along_y
    )
    sends += exchange(
        f_ref.at[pl.ds(base, 4)],
        [f_ref.at[pl.ds(core * 16 + ((x + 4 - d) % NX) * 4, 4)] for d in range(1, 4)],
        x_send, x_recv, along_x,
    )
    sends += exchange(
        f_ref.at[pl.ds(core * 16, 16)], [f_ref.at[pl.ds((1 - core) * 16, 16)]], c_send, c_recv, [partner]
    )
    for copy in sends:
        copy.wait_send()


def gather_features(own, other, targets):
    size = own.shape[1]
    inside = pl.BlockSpec(memory_space=pltpu.VMEM)
    sem = pltpu.SemaphoreType.DMA
    return pl.pallas_call(
        features_kernel,
        out_shape=jax.ShapeDtypeStruct((32, 32, size + 128), jnp.bfloat16),
        in_specs=[inside] * 3,
        out_specs=inside,
        scratch_shapes=[
            pltpu.VMEM((2, size), jnp.float32),
            pltpu.VMEM((NZ, 2, size + 128), jnp.bfloat16),
            pltpu.VMEM((32, size + 128), jnp.float32),
            sem, sem, sem((3,)), sem((3,)), sem((3,)), sem((3,)), sem((3,)), sem((3,)),
            sem((3,)), sem((3,)), sem((1,)), sem((1,)),
        ],
        compiler_params=pltpu.CompilerParams(collective_id=1, has_side_effects=True),
        name="gather_features",
    )(own, other, targets)


def invert(m):
    side = m.shape[0]
    lane = lax.broadcasted_iota(jnp.int32, m.shape, 1)
    sub = lax.broadcasted_iota(jnp.int32, m.shape, 0)
    for k in range(0, side, 2):
        j = k + 1
        c0 = jnp.broadcast_to(m[:, k:k + 1], m.shape)
        c1 = jnp.broadcast_to(m[:, j:j + 1], m.shape)
        inv0 = 1.0 / c0[k:k + 1, :]
        r0 = jnp.where(lane[0:1] == k, 1.0, m[k:k + 1, :]) * inv0
        r1 = jnp.where(lane[0:1] == k, 0.0, m[j:j + 1, :]) - c0[j:j + 1, :] * r0
        across = c1[k:k + 1, :] * inv0
        inv1 = 1.0 / (c1[j:j + 1, :] - c0[j:j + 1, :] * across)
        r1 = jnp.where(lane[0:1] == j, 1.0, r1) * inv1
        c0 = jnp.where(sub == k, -1.0, c0)
        c1 = jnp.where(sub == k, 0.0, c1) - c0 * across
        c1 = jnp.where(sub == j, -1.0, c1)
        m = jnp.where((lane == k) | (sub == k), 0.0, m) - c0 * r0
        m = jnp.where((lane == j) | (sub == j), 0.0, m) - c1 * r1
    return m


def solve_kernel(a_ref, out_ref, work):
    size = a_ref.shape[0]
    side = 128
    high = lax.Precision.HIGHEST
    diagonal = lax.broadcasted_iota(jnp.int32, a_ref.shape, 0) == lax.broadcasted_iota(jnp.int32, a_ref.shape, 1)
    work[...] = a_ref[...] + jnp.where(diagonal, DAMPING, 0.0)

    def body(block, carry):
        here = pl.ds(pl.multiple_of(block * side, side), side)
        rows = jnp.dot(invert(work[here, here]), work[here, :], precision=high, preferred_element_type=jnp.float32)
        work[...] = work[...] - jnp.dot(work[:, here], rows, precision=high, preferred_element_type=jnp.float32)
        work[here, :] = rows
        return carry

    lax.fori_loop(0, size // side, body, 0)
    out_ref[...] = lax.dot_general(
        jnp.ones((8, a_ref.shape[1] - size), jnp.float32),
        work[:, size:],
        (((1,), (1,)), ((), ())),
        precision=high,
        preferred_element_type=jnp.float32,
    )


def solve(extended):
    return pl.pallas_call(
        solve_kernel,
        out_shape=jax.ShapeDtypeStruct((8, extended.shape[0]), jnp.float32),
        in_specs=[pl.BlockSpec(memory_space=pltpu.VMEM)],
        out_specs=pl.BlockSpec(memory_space=pltpu.VMEM),
        scratch_shapes=[pltpu.VMEM(extended.shape, jnp.float32)],
        name="solve",
    )(extended)[0]


def block_kernel(
    x_ref, g_ref, other_x_ref, other_g_ref, w_ref, sketch_ref, sketch_in_ref, out_ref, hq_ref, dq_ref
):
    step = pl.program_id(0)
    length = x_ref.shape[1]

    @pl.when(step == 0)
    def _():
        hq_ref[...] = jnp.zeros_like(hq_ref)
        dq_ref[...] = jnp.zeros_like(dq_ref)

    pairs = [(x_ref, g_ref, 0), (x_ref, g_ref, 1), (other_x_ref, other_g_ref, 0), (other_x_ref, other_g_ref, 1)]
    sketch = sketch_ref[...]
    across = (((1,), (1,)), ((), ()))
    for n, (xs, gs, at) in enumerate(pairs):
        pre = lax.dot_general(xs[at], w_ref[0], across, preferred_element_type=jnp.float32)
        back = lax.dot_general(gs[at], w_ref[1], across, preferred_element_type=jnp.float32)
        sig = jax.nn.sigmoid(pre)
        hidden = (pre * sig).astype(jnp.bfloat16)
        slope = (back * sig * (1.0 + pre * (1.0 - sig))).astype(jnp.bfloat16)
        hq_ref[n] += jnp.dot(hidden, sketch, preferred_element_type=jnp.float32)
        dq_ref[n] += jnp.dot(slope, sketch, preferred_element_type=jnp.float32)

    @pl.when(step == pl.num_programs(0) - 1)
    def _():
        for n, (xs, gs, at) in enumerate(pairs):
            xp = jnp.dot(xs[at], sketch_in_ref[...], preferred_element_type=jnp.float32)
            gp = jnp.dot(gs[at], sketch_in_ref[...], preferred_element_type=jnp.float32)
            for which, (left, right) in enumerate([(dq_ref[n], xp), (hq_ref[n], gp)]):
                out_ref[n, which] = lax.dot_general(
                    left, right, (((0,), (0,)), ((), ())),
                    precision=lax.Precision.HIGHEST, preferred_element_type=jnp.float32,
                ) * (1.0 / length)


def partial_features(samples, cotangent, other_x, other_g, weights, sketch_rows, sketch_in):
    count, length, width = samples.shape
    hidden_units, rank = sketch_rows.shape
    chunk = 256
    whole = pl.BlockSpec((count, length, width), lambda i: (0, 0, 0))
    return pl.pallas_call(
        block_kernel,
        grid=(hidden_units // chunk,),
        out_shape=jax.ShapeDtypeStruct((2 * count, 2, rank, rank), jnp.float32),
        in_specs=[whole] * 4 + [
            pl.BlockSpec((2, chunk, width), lambda i: (0, i, 0)),
            pl.BlockSpec((chunk, rank), lambda i: (i, 0)),
            pl.BlockSpec((width, rank), lambda i: (0, 0)),
        ],
        out_specs=pl.BlockSpec((2 * count, 2, rank, rank), lambda i: (0, 0, 0, 0)),
        scratch_shapes=[
            pltpu.VMEM((2 * count, length, rank), jnp.float32),
            pltpu.VMEM((2 * count, length, rank), jnp.float32),
        ],
        compiler_params=pltpu.CompilerParams(vmem_limit_bytes=48 * 2**20),
        name="pointwise_block",
    )(samples, cotangent, other_x, other_g, weights, sketch_rows, sketch_in)


def per_device(samples, cotangent, w_in, w_out, sketch_in, sketch_hidden, targets):
    count, length, width = samples.shape
    rows = w_in.shape[0]
    weights, other_x, other_g = gather_weights(samples, cotangent, w_in, w_out)
    core = lax.axis_index("fsdp") % 2
    sketch_rows = lax.dynamic_index_in_dim(
        sketch_hidden.reshape(NZ * 2, 2, rows, -1), core, 1, keepdims=False
    ).reshape(NZ * 2 * rows, -1)
    partial = partial_features(
        samples, cotangent, other_x, other_g, weights.reshape(2, -1, width), sketch_rows, sketch_in
    ).reshape(2 * count, -1)
    own, other = partial[:count], partial[count:]
    table = gather_features(own, other, targets.reshape(count, 1))
    size = own.shape[1]
    table = table.reshape(-1, size + 128)
    everyone = table[:, :size]
    extended = lax.dot_general(
        everyone, table, (((0,), (0,)), ((), ())), preferred_element_type=jnp.float32
    )
    step = solve(extended)
    x, y, z, core = position()
    start = (core * 16 + x * 4 + y) * 32 + z * count
    feats = lax.dynamic_slice_in_dim(everyone, start, count, 0)
    fitted = jnp.dot(feats.astype(jnp.float32), step, precision=lax.Precision.HIGHEST)
    coeffs = (targets - fitted) / DAMPING
    return (coeffs, step)


def solution(mesh):
    in_specs = (
        P(("dp", "fsdp"), None, None),
        P(("dp", "fsdp"), None, None),
        P("fsdp", None),
        P("fsdp", None),
        P(),
        P(),
        P(("dp", "fsdp")),
    )
    out_specs = (P(("dp", "fsdp")), P())
    return jax.shard_map(
        per_device, mesh=mesh, in_specs=in_specs, out_specs=out_specs, check_vma=False
    )
```

```python
import jax
import jax.numpy as jnp
from jax import lax
from jax.experimental import pallas as pl
from jax.experimental.pallas import tpu as pltpu
from jax.sharding import PartitionSpec as P

DAMPING = 0.5
NZ, NY, NX = 16, 4, 4
MESH = pl.DeviceIdType.MESH


def position():
    group, member = lax.axis_index("dp"), lax.axis_index("fsdp")
    x = (group // 4) * 2 + (member // 2) % 2
    return x, group % 4, member // 4, member % 2


def device(x, y, z, core):
    return ((x // 2) * 4 + y, z * 4 + (x % 2) * 2 + core)


def greet(partners):
    barrier = pltpu.get_barrier_semaphore()
    for partner in partners:
        pl.semaphore_signal(barrier, inc=1, device_id=partner, device_id_type=MESH)
    pl.semaphore_wait(barrier, len(partners))


def weights_kernel(
    x_ref, g_ref, w_ref, all_ref, px_ref, pg_ref,
    swap_send, swap_recv, local_sem, z_send, z_recv, y_send, y_recv, o_send, o_recv, x_send, x_recv,
):
    x, y, z, core = position()
    low = x % 2
    up, down = (z + 1) % NZ, (z + NZ - 1) % NZ
    y_up, y_down = (y + 1) % NY, (y + NY - 1) % NY
    x_up, x_down = (x + 1) % NX, (x + NX - 1) % NX
    greet([
        device(x, y, up, core), device(x, y, down, core),
        device(x, y_up, z, core), device(x, y_down, z, core),
        device(x_up, y, z, core), device(x_down, y, z, core),
        device(x, y, z, 1 - core),
    ])
    sends = []

    def place(zz, q, lo):
        return all_ref.at[q // 2, zz, lo, q % 2]

    def remote(src, dst, send, recv, target):
        return pltpu.make_async_remote_copy(
            src_ref=src, dst_ref=dst, send_sem=send, recv_sem=recv, device_id=target, device_id_type=MESH
        )

    def start(copy):
        copy.start()
        sends.append(copy)

    def send_x(src, zz, q):
        target = device((x + (q // 2) * 2 + NX - 1) % NX, y, z, core)
        start(remote(src, place(zz, q, low), x_send.at[zz, q], x_recv.at[zz, q], target))

    def send_y(src, zz):
        start(remote(src, place(zz, y, low), y_send.at[0, zz], y_recv.at[0, zz], device(x, y_up, z, core)))
        start(remote(src, place(zz, y, low), y_send.at[1, zz], y_recv.at[1, zz], device(x, y_down, z, core)))

    def wait_recv(dst, recv):
        remote(dst, dst, swap_send.at[0], recv, device(x, y, z, 1 - core)).wait_recv()

    mine = w_ref.at[y // 2, y % 2]
    start(remote(mine, place(z, y, low), z_send.at[0, 1], z_recv.at[0, 1], device(x, y, up, core)))
    start(remote(mine, place(z, y, low), z_send.at[1, 1], z_recv.at[1, 1], device(x, y, down, core)))
    for q in range(4):
        send_x(w_ref.at[q // 2, q % 2], z, q)
    locals_ = []
    for q in range(4):
        copy = pltpu.make_async_copy(w_ref.at[q // 2, q % 2], place(z, q, low), local_sem.at[q])
        copy.start()
        locals_.append(copy)
    start(remote(x_ref, px_ref, swap_send.at[0], swap_recv.at[0], device(x, y, z, 1 - core)))
    start(remote(g_ref, pg_ref, swap_send.at[1], swap_recv.at[1], device(x, y, z, 1 - core)))

    def blocks_of(step):
        found = []
        if 1 <= step <= 8:
            found.append((0, (z + NZ - step) % NZ))
        if 1 <= step <= 7:
            found.append((1, (z + step) % NZ))
        return found

    for step in range(1, 12):
        for way, zz in blocks_of(step):
            here = place(zz, y, low)
            wait_recv(here, z_recv.at[way, step])
            if step < (8 if way == 0 else 7):
                target = device(x, y, up if way == 0 else down, core)
                start(remote(here, here, z_send.at[way, step + 1], z_recv.at[way, step + 1], target))
            send_y(here, zz)
            send_x(here, zz, y)
        for way, zz in blocks_of(step - 2):
            below, above = place(zz, y_down, low), place(zz, y_up, low)
            wait_recv(below, y_recv.at[0, zz])
            wait_recv(above, y_recv.at[1, zz])
            if way == 0:
                start(remote(below, below, o_send.at[zz], o_recv.at[zz], device(x, y_up, z, core)))
            else:
                start(remote(above, above, o_send.at[zz], o_recv.at[zz], device(x, y_down, z, core)))
            send_x(below, zz, y_down)
            send_x(above, zz, y_up)
        for way, zz in blocks_of(step - 3):
            far = (y + 2) % NY
            wait_recv(place(zz, far, low), o_recv.at[zz])
            send_x(place(zz, far, low), zz, far)
    for zz in range(NZ):
        for q in range(4):
            wait_recv(place(zz, q, 1 - low), x_recv.at[zz, q])
    wait_recv(px_ref, swap_recv.at[0])
    wait_recv(pg_ref, swap_recv.at[1])
    for copy in locals_:
        copy.wait()
    for copy in sends:
        copy.wait_send()


def gather_weights(flat_x, flat_g, w_in, w_out):
    rows, width = w_in.shape
    half = rows // 2
    w = jnp.stack([w_in, w_out]).reshape(2, 2, half, width)
    anywhere = pl.BlockSpec(memory_space=pl.ANY)
    sem = pltpu.SemaphoreType.DMA
    return pl.pallas_call(
        weights_kernel,
        out_shape=(
            jax.ShapeDtypeStruct((2, NZ, 2, 2, half, width), w.dtype),
            jax.ShapeDtypeStruct(flat_x.shape, flat_x.dtype),
            jax.ShapeDtypeStruct(flat_g.shape, flat_g.dtype),
        ),
        in_specs=[anywhere] * 3,
        out_specs=(anywhere,) * 3,
        scratch_shapes=[
            sem((2,)), sem((2,)), sem((4,)), sem((2, 9)), sem((2, 9)), sem((2, NZ)), sem((2, NZ)),
            sem((NZ,)), sem((NZ,)), sem((NZ, 4)), sem((NZ, 4)),
        ],
        compiler_params=pltpu.CompilerParams(collective_id=0, has_side_effects=True),
        name="gather_weights",
    )(flat_x, flat_g, w)


def features_kernel(
    own_ref, other_ref, targets_ref, f_ref, got, zbuf, wide,
    swap_send, swap_recv, z_send, z_recv, y_send, y_recv, x_send, x_recv, c_send, c_recv,
):
    x, y, z, core = position()
    along_z = [device(x, y, (z + d) % NZ, core) for d in range(1, NZ)]
    along_y = [device(x, (y + d) % NY, z, core) for d in range(1, 4)]
    along_x = [device((x + d) % NX, y, z, core) for d in range(1, 4)]
    partner = device(x, y, z, 1 - core)
    greet(along_z + along_y + along_x + [partner])

    def remote(src, dst, send, recv, target):
        return pltpu.make_async_remote_copy(
            src_ref=src, dst_ref=dst, send_sem=send, recv_sem=recv, device_id=target, device_id_type=MESH
        )

    def begin(mine, send, recv, partners):
        copies = []
        for d, target in enumerate(partners):
            copy = remote(mine, mine, send.at[d], recv.at[d], target)
            copy.start()
            copies.append(copy)
        return copies

    def finish(theirs, send, recv, partners):
        for d, target in enumerate(partners):
            remote(theirs[d], theirs[d], send.at[d], recv.at[d], target).wait_recv()

    swap = remote(other_ref, got, swap_send, swap_recv, partner)
    swap.start()
    swap.wait_recv()
    feats = own_ref[...] + got[...]
    t = targets_ref[...]
    high_t = t.astype(jnp.bfloat16).astype(jnp.float32)
    mid_t = (t - high_t).astype(jnp.bfloat16).astype(jnp.float32)
    low_t = t - high_t - mid_t
    lane = lax.broadcasted_iota(jnp.int32, (2, 128), 1)
    tail = jnp.where(lane == 0, high_t, jnp.where(lane == 1, mid_t, jnp.where(lane == 2, low_t, 0.0)))
    size = feats.shape[1]
    zbuf[z, :, 0:size] = feats.astype(jnp.bfloat16)
    zbuf[z, :, size:] = tail.astype(jnp.bfloat16)
    sends = [swap]
    sends += begin(zbuf.at[z], z_send, z_recv, along_z)
    finish([zbuf.at[(z + NZ - d) % NZ] for d in range(1, NZ)], z_send, z_recv, along_z)
    for zz in range(NZ):
        wide[2 * zz:2 * zz + 2, :] = zbuf[zz].astype(jnp.float32)
    packed = wide[...].astype(jnp.bfloat16)
    f_ref[core, x, y, 0] = packed[0:NZ]
    f_ref[core, x, y, 1] = packed[NZ:]
    ys = [(y + 4 - d) % NY for d in range(1, 4)]
    xs = [(x + 4 - d) % NX for d in range(1, 4)]
    sends += begin(f_ref.at[core, x, y, 0], y_send.at[0], y_recv.at[0], along_y)
    sends += begin(f_ref.at[core, x, y, 1], x_send.at[0], x_recv.at[0], along_x)
    finish([f_ref.at[core, x, yy, 0] for yy in ys], y_send.at[0], y_recv.at[0], along_y)
    sends += begin(f_ref.at[core, x, :, 0], x_send.at[1], x_recv.at[1], along_x)
    finish([f_ref.at[core, xx, y, 1] for xx in xs], x_send.at[0], x_recv.at[0], along_x)
    sends += begin(f_ref.at[core, :, y, 1], y_send.at[1], y_recv.at[1], along_y)
    finish([f_ref.at[core, xx, :, 0] for xx in xs], x_send.at[1], x_recv.at[1], along_x)
    finish([f_ref.at[core, :, yy, 1] for yy in ys], y_send.at[1], y_recv.at[1], along_y)
    sends += begin(f_ref.at[core], c_send, c_recv, [partner])
    finish([f_ref.at[1 - core]], c_send, c_recv, [partner])
    for copy in sends:
        copy.wait_send()


def gather_features(own, other, targets):
    size = own.shape[1]
    inside = pl.BlockSpec(memory_space=pltpu.VMEM)
    sem = pltpu.SemaphoreType.DMA
    return pl.pallas_call(
        features_kernel,
        out_shape=jax.ShapeDtypeStruct((2, NX, NY, 2, NZ, size + 128), jnp.bfloat16),
        in_specs=[inside] * 3,
        out_specs=inside,
        scratch_shapes=[
            pltpu.VMEM((2, size), jnp.float32),
            pltpu.VMEM((NZ, 2, size + 128), jnp.bfloat16),
            pltpu.VMEM((32, size + 128), jnp.float32),
            sem, sem, sem((NZ - 1,)), sem((NZ - 1,)), sem((2, 3)), sem((2, 3)), sem((2, 3)), sem((2, 3)),
            sem((1,)), sem((1,)),
        ],
        compiler_params=pltpu.CompilerParams(collective_id=1, has_side_effects=True),
        name="gather_features",
    )(own, other, targets)


def invert(m, width=8):
    side = m.shape[0]
    lane = lax.broadcasted_iota(jnp.int32, m.shape, 1)
    sub = lax.broadcasted_iota(jnp.int32, m.shape, 0)
    for k in range(0, side, width):
        columns = [jnp.broadcast_to(m[:, k + i:k + i + 1], m.shape) for i in range(width)]
        rows = [m[k + i:k + i + 1, :] for i in range(width)]
        for i in range(width):
            at = k + i
            column = columns[i]
            inverse = 1.0 / column[at:at + 1, :]
            row = jnp.where(lane[0:1] == at, 1.0, rows[i]) * inverse
            swept = jnp.where(sub == at, -1.0, column)
            for j in range(i + 1, width):
                to = k + j
                rows[j] = jnp.where(lane[0:1] == at, 0.0, rows[j]) - column[to:to + 1, :] * row
                columns[j] = jnp.where(sub == at, 0.0, columns[j]) - swept * (columns[j][at:at + 1, :] * inverse)
            m = jnp.where((lane == at) | (sub == at), 0.0, m) - swept * row
    return m


def solve_kernel(a_ref, out_ref, work):
    size = a_ref.shape[0]
    side = 128
    high = lax.Precision.HIGHEST
    diagonal = lax.broadcasted_iota(jnp.int32, a_ref.shape, 0) == lax.broadcasted_iota(jnp.int32, a_ref.shape, 1)
    work[...] = a_ref[...] + jnp.where(diagonal, DAMPING, 0.0)

    def body(block, carry):
        here = pl.ds(pl.multiple_of(block * side, side), side)
        rows = jnp.dot(invert(work[here, here]), work[here, :], precision=high, preferred_element_type=jnp.float32)
        work[...] = work[...] - jnp.dot(work[:, here], rows, precision=high, preferred_element_type=jnp.float32)
        work[here, :] = rows
        return carry

    lax.fori_loop(0, size // side, body, 0)
    out_ref[...] = lax.dot_general(
        jnp.ones((8, a_ref.shape[1] - size), jnp.float32),
        work[:, size:],
        (((1,), (1,)), ((), ())),
        precision=high,
        preferred_element_type=jnp.float32,
    )


def solve(extended):
    return pl.pallas_call(
        solve_kernel,
        out_shape=jax.ShapeDtypeStruct((8, extended.shape[0]), jnp.float32),
        in_specs=[pl.BlockSpec(memory_space=pltpu.VMEM)],
        out_specs=pl.BlockSpec(memory_space=pltpu.VMEM),
        scratch_shapes=[pltpu.VMEM(extended.shape, jnp.float32)],
        name="solve",
    )(extended)[0]


def block_kernel(
    x_ref, g_ref, other_x_ref, other_g_ref, w_ref, sketch_ref, sketch_in_ref, out_ref, hq_ref, dq_ref
):
    step = pl.program_id(0)
    length = x_ref.shape[1]

    @pl.when(step == 0)
    def _():
        hq_ref[...] = jnp.zeros_like(hq_ref)
        dq_ref[...] = jnp.zeros_like(dq_ref)

    pairs = [(x_ref, g_ref, 0), (x_ref, g_ref, 1), (other_x_ref, other_g_ref, 0), (other_x_ref, other_g_ref, 1)]
    sketch = sketch_ref[...]
    across = (((1,), (1,)), ((), ()))
    for n, (xs, gs, at) in enumerate(pairs):
        pre = lax.dot_general(xs[at], w_ref[0], across, preferred_element_type=jnp.float32)
        back = lax.dot_general(gs[at], w_ref[1], across, preferred_element_type=jnp.float32)
        sig = jax.nn.sigmoid(pre)
        hidden = (pre * sig).astype(jnp.bfloat16)
        slope = (back * sig * (1.0 + pre * (1.0 - sig))).astype(jnp.bfloat16)
        hq_ref[n] += jnp.dot(hidden, sketch, preferred_element_type=jnp.float32)
        dq_ref[n] += jnp.dot(slope, sketch, preferred_element_type=jnp.float32)

    @pl.when(step == pl.num_programs(0) - 1)
    def _():
        for n, (xs, gs, at) in enumerate(pairs):
            xp = jnp.dot(xs[at], sketch_in_ref[...], preferred_element_type=jnp.float32)
            gp = jnp.dot(gs[at], sketch_in_ref[...], preferred_element_type=jnp.float32)
            for which, (left, right) in enumerate([(dq_ref[n], xp), (hq_ref[n], gp)]):
                out_ref[n, which] = lax.dot_general(
                    left, right, (((0,), (0,)), ((), ())),
                    precision=lax.Precision.HIGHEST, preferred_element_type=jnp.float32,
                ) * (1.0 / length)


def partial_features(samples, cotangent, other_x, other_g, weights, sketch_rows, sketch_in):
    count, length, width = samples.shape
    hidden_units, rank = sketch_rows.shape
    chunk = 256
    whole = pl.BlockSpec((count, length, width), lambda i: (0, 0, 0))
    return pl.pallas_call(
        block_kernel,
        grid=(hidden_units // chunk,),
        out_shape=jax.ShapeDtypeStruct((2 * count, 2, rank, rank), jnp.float32),
        in_specs=[whole] * 4 + [
            pl.BlockSpec((2, chunk, width), lambda i: (0, i, 0)),
            pl.BlockSpec((chunk, rank), lambda i: (i, 0)),
            pl.BlockSpec((width, rank), lambda i: (0, 0)),
        ],
        out_specs=pl.BlockSpec((2 * count, 2, rank, rank), lambda i: (0, 0, 0, 0)),
        scratch_shapes=[
            pltpu.VMEM((2 * count, length, rank), jnp.float32),
            pltpu.VMEM((2 * count, length, rank), jnp.float32),
        ],
        compiler_params=pltpu.CompilerParams(vmem_limit_bytes=48 * 2**20),
        name="pointwise_block",
    )(samples, cotangent, other_x, other_g, weights, sketch_rows, sketch_in)


def per_device(samples, cotangent, w_in, w_out, sketch_in, sketch_hidden, targets):
    count, length, width = samples.shape
    rows = w_in.shape[0]
    weights, other_x, other_g = gather_weights(samples, cotangent, w_in, w_out)
    core = lax.axis_index("fsdp") % 2
    sketch_rows = lax.dynamic_index_in_dim(
        sketch_hidden.reshape(NZ * 2, 2, rows, -1), core, 1, keepdims=False
    ).reshape(NZ * 2 * rows, -1)
    partial = partial_features(
        samples, cotangent, other_x, other_g, weights.reshape(2, -1, width), sketch_rows, sketch_in
    ).reshape(2 * count, -1)
    own, other = partial[:count], partial[count:]
    table = gather_features(own, other, targets.reshape(count, 1))
    size = own.shape[1]
    table = table.reshape(-1, size + 128)
    everyone = table[:, :size]
    extended = lax.dot_general(
        everyone, table, (((0,), (0,)), ((), ())), preferred_element_type=jnp.float32
    )
    step = solve(extended)
    x, y, z, core = position()
    start = (core * 16 + x * 4 + y) * 32 + z * count
    feats = lax.dynamic_slice_in_dim(everyone, start, count, 0)
    fitted = jnp.dot(feats.astype(jnp.float32), step, precision=lax.Precision.HIGHEST)
    coeffs = (targets - fitted) / DAMPING
    return (coeffs, step)


def solution(mesh):
    in_specs = (
        P(("dp", "fsdp"), None, None),
        P(("dp", "fsdp"), None, None),
        P("fsdp", None),
        P("fsdp", None),
        P(),
        P(),
        P(("dp", "fsdp")),
    )
    out_specs = (P(("dp", "fsdp")), P())
    return jax.shard_map(
        per_device, mesh=mesh, in_specs=in_specs, out_specs=out_specs, check_vma=False
    )
```

```python
import jax
import jax.numpy as jnp
from jax import lax
from jax.experimental import pallas as pl
from jax.experimental.pallas import tpu as pltpu
from jax.sharding import PartitionSpec as P

DAMPING = 0.5
NZ, NY, NX = 16, 4, 4
MESH = pl.DeviceIdType.MESH


def position():
    group, member = lax.axis_index("dp"), lax.axis_index("fsdp")
    x = (group // 4) * 2 + (member // 2) % 2
    return x, group % 4, member // 4, member % 2


def device(x, y, z, core):
    return ((x // 2) * 4 + y, z * 4 + (x % 2) * 2 + core)


def greet(partners):
    barrier = pltpu.get_barrier_semaphore()
    for partner in partners:
        pl.semaphore_signal(barrier, inc=1, device_id=partner, device_id_type=MESH)
    pl.semaphore_wait(barrier, len(partners))


def weights_kernel(
    x_ref, g_ref, w_ref, all_ref, px_ref, pg_ref,
    swap_send, swap_recv, local_sem, z_send, z_recv, y_send, y_recv, o_send, o_recv, x_send, x_recv,
):
    x, y, z, core = position()
    low = x % 2
    up, down = (z + 1) % NZ, (z + NZ - 1) % NZ
    up2, down2 = (z + 2) % NZ, (z + NZ - 2) % NZ
    y_up, y_down = (y + 1) % NY, (y + NY - 1) % NY
    x_up, x_down = (x + 1) % NX, (x + NX - 1) % NX
    greet([
        device(x, y, up, core), device(x, y, down, core),
        device(x, y, up2, core), device(x, y, down2, core),
        device(x, y_up, z, core), device(x, y_down, z, core),
        device(x_up, y, z, core), device(x_down, y, z, core),
        device(x, y, z, 1 - core),
    ])
    sends = []

    def place(zz, q, lo):
        return all_ref.at[q // 2, zz, lo, q % 2]

    def remote(src, dst, send, recv, target):
        return pltpu.make_async_remote_copy(
            src_ref=src, dst_ref=dst, send_sem=send, recv_sem=recv, device_id=target, device_id_type=MESH
        )

    def start(copy):
        copy.start()
        sends.append(copy)

    def send_x(src, zz, q):
        target = device((x + (q // 2) * 2 + NX - 1) % NX, y, z, core)
        start(remote(src, place(zz, q, low), x_send.at[zz, q], x_recv.at[zz, q], target))

    def send_y(src, zz):
        start(remote(src, place(zz, y, low), y_send.at[0, zz], y_recv.at[0, zz], device(x, y_up, z, core)))
        start(remote(src, place(zz, y, low), y_send.at[1, zz], y_recv.at[1, zz], device(x, y_down, z, core)))

    def wait_recv(dst, recv):
        remote(dst, dst, swap_send.at[0], recv, device(x, y, z, 1 - core)).wait_recv()

    mine = w_ref.at[y // 2, y % 2]
    start(remote(mine, place(z, y, low), z_send.at[0, 1], z_recv.at[0, 1], device(x, y, up, core)))
    start(remote(mine, place(z, y, low), z_send.at[1, 1], z_recv.at[1, 1], device(x, y, down, core)))
    start(remote(mine, place(z, y, low), z_send.at[0, 2], z_recv.at[0, 2], device(x, y, up2, core)))
    start(remote(mine, place(z, y, low), z_send.at[1, 2], z_recv.at[1, 2], device(x, y, down2, core)))
    for q in range(4):
        send_x(w_ref.at[q // 2, q % 2], z, q)
    locals_ = []
    for q in range(4):
        copy = pltpu.make_async_copy(w_ref.at[q // 2, q % 2], place(z, q, low), local_sem.at[q])
        copy.start()
        locals_.append(copy)
    start(remote(x_ref, px_ref, swap_send.at[0], swap_recv.at[0], device(x, y, z, 1 - core)))
    start(remote(g_ref, pg_ref, swap_send.at[1], swap_recv.at[1], device(x, y, z, 1 - core)))

    def blocks_of(step):
        found = []
        if 1 <= step <= 8:
            found.append((0, (z + NZ - step) % NZ))
        if 1 <= step <= 7:
            found.append((1, (z + step) % NZ))
        return found

    for step in range(1, 12):
        for way, zz in blocks_of(step):
            here = place(zz, y, low)
            wait_recv(here, z_recv.at[way, step])
            if step + 2 <= (8 if way == 0 else 7):
                target = device(x, y, up2 if way == 0 else down2, core)
                start(remote(here, here, z_send.at[way, step + 2], z_recv.at[way, step + 2], target))
            send_y(here, zz)
            send_x(here, zz, y)
        for way, zz in blocks_of(step - 2):
            below, above = place(zz, y_down, low), place(zz, y_up, low)
            wait_recv(below, y_recv.at[0, zz])
            wait_recv(above, y_recv.at[1, zz])
            if way == 0:
                start(remote(below, below, o_send.at[zz], o_recv.at[zz], device(x, y_up, z, core)))
            else:
                start(remote(above, above, o_send.at[zz], o_recv.at[zz], device(x, y_down, z, core)))
            send_x(below, zz, y_down)
            send_x(above, zz, y_up)
        for way, zz in blocks_of(step - 3):
            far = (y + 2) % NY
            wait_recv(place(zz, far, low), o_recv.at[zz])
            send_x(place(zz, far, low), zz, far)
    for zz in range(NZ):
        for q in range(4):
            wait_recv(place(zz, q, 1 - low), x_recv.at[zz, q])
    wait_recv(px_ref, swap_recv.at[0])
    wait_recv(pg_ref, swap_recv.at[1])
    for copy in locals_:
        copy.wait()
    for copy in sends:
        copy.wait_send()


def gather_weights(flat_x, flat_g, w_in, w_out):
    rows, width = w_in.shape
    half = rows // 2
    w = jnp.stack([w_in, w_out]).reshape(2, 2, half, width)
    anywhere = pl.BlockSpec(memory_space=pl.ANY)
    sem = pltpu.SemaphoreType.DMA
    return pl.pallas_call(
        weights_kernel,
        out_shape=(
            jax.ShapeDtypeStruct((2, NZ, 2, 2, half, width), w.dtype),
            jax.ShapeDtypeStruct(flat_x.shape, flat_x.dtype),
            jax.ShapeDtypeStruct(flat_g.shape, flat_g.dtype),
        ),
        in_specs=[anywhere] * 3,
        out_specs=(anywhere,) * 3,
        scratch_shapes=[
            sem((2,)), sem((2,)), sem((4,)), sem((2, 9)), sem((2, 9)), sem((2, NZ)), sem((2, NZ)),
            sem((NZ,)), sem((NZ,)), sem((NZ, 4)), sem((NZ, 4)),
        ],
        compiler_params=pltpu.CompilerParams(collective_id=0, has_side_effects=True),
        name="gather_weights",
    )(flat_x, flat_g, w)


def features_kernel(
    own_ref, other_ref, targets_ref, f_ref, got, zbuf, wide,
    swap_send, swap_recv, z_send, z_recv, y_send, y_recv, x_send, x_recv, c_send, c_recv,
):
    x, y, z, core = position()
    along_z = [device(x, y, (z + d) % NZ, core) for d in range(1, NZ)]
    along_y = [device(x, (y + d) % NY, z, core) for d in range(1, 4)]
    along_x = [device((x + d) % NX, y, z, core) for d in range(1, 4)]
    partner = device(x, y, z, 1 - core)
    greet(along_z + along_y + along_x + [partner])

    def remote(src, dst, send, recv, target):
        return pltpu.make_async_remote_copy(
            src_ref=src, dst_ref=dst, send_sem=send, recv_sem=recv, device_id=target, device_id_type=MESH
        )

    def begin(mine, send, recv, partners):
        copies = []
        for d, target in enumerate(partners):
            copy = remote(mine, mine, send.at[d], recv.at[d], target)
            copy.start()
            copies.append(copy)
        return copies

    def finish(theirs, send, recv, partners):
        for d, target in enumerate(partners):
            remote(theirs[d], theirs[d], send.at[d], recv.at[d], target).wait_recv()

    swap = remote(other_ref, got, swap_send, swap_recv, partner)
    swap.start()
    swap.wait_recv()
    feats = own_ref[...] + got[...]
    t = targets_ref[...]
    high_t = t.astype(jnp.bfloat16).astype(jnp.float32)
    mid_t = (t - high_t).astype(jnp.bfloat16).astype(jnp.float32)
    low_t = t - high_t - mid_t
    lane = lax.broadcasted_iota(jnp.int32, (2, 128), 1)
    tail = jnp.where(lane == 0, high_t, jnp.where(lane == 1, mid_t, jnp.where(lane == 2, low_t, 0.0)))
    size = feats.shape[1]
    zbuf[z, :, 0:size] = feats.astype(jnp.bfloat16)
    zbuf[z, :, size:] = tail.astype(jnp.bfloat16)
    sends = [swap]
    sends += begin(zbuf.at[z], z_send, z_recv, along_z)
    finish([zbuf.at[(z + NZ - d) % NZ] for d in range(1, NZ)], z_send, z_recv, along_z)
    for zz in range(NZ):
        wide[2 * zz:2 * zz + 2, :] = zbuf[zz].astype(jnp.float32)
    packed = wide[...].astype(jnp.bfloat16)
    f_ref[core, x, y, 0] = packed[0:NZ]
    f_ref[core, x, y, 1] = packed[NZ:]
    ys = [(y + 4 - d) % NY for d in range(1, 4)]
    xs = [(x + 4 - d) % NX for d in range(1, 4)]
    sends += begin(f_ref.at[core, x, y, 0], y_send.at[0], y_recv.at[0], along_y)
    sends += begin(f_ref.at[core, x, y, 1], x_send.at[0], x_recv.at[0], along_x)
    finish([f_ref.at[core, x, yy, 0] for yy in ys], y_send.at[0], y_recv.at[0], along_y)
    sends += begin(f_ref.at[core, x, :, 0], x_send.at[1], x_recv.at[1], along_x)
    finish([f_ref.at[core, xx, y, 1] for xx in xs], x_send.at[0], x_recv.at[0], along_x)
    sends += begin(f_ref.at[core, :, y, 1], y_send.at[1], y_recv.at[1], along_y)
    finish([f_ref.at[core, xx, :, 0] for xx in xs], x_send.at[1], x_recv.at[1], along_x)
    finish([f_ref.at[core, :, yy, 1] for yy in ys], y_send.at[1], y_recv.at[1], along_y)
    sends += begin(f_ref.at[core], c_send, c_recv, [partner])
    finish([f_ref.at[1 - core]], c_send, c_recv, [partner])
    for copy in sends:
        copy.wait_send()


def gather_features(own, other, targets):
    size = own.shape[1]
    inside = pl.BlockSpec(memory_space=pltpu.VMEM)
    sem = pltpu.SemaphoreType.DMA
    return pl.pallas_call(
        features_kernel,
        out_shape=jax.ShapeDtypeStruct((2, NX, NY, 2, NZ, size + 128), jnp.bfloat16),
        in_specs=[inside] * 3,
        out_specs=inside,
        scratch_shapes=[
            pltpu.VMEM((2, size), jnp.float32),
            pltpu.VMEM((NZ, 2, size + 128), jnp.bfloat16),
            pltpu.VMEM((32, size + 128), jnp.float32),
            sem, sem, sem((NZ - 1,)), sem((NZ - 1,)), sem((2, 3)), sem((2, 3)), sem((2, 3)), sem((2, 3)),
            sem((1,)), sem((1,)),
        ],
        compiler_params=pltpu.CompilerParams(collective_id=1, has_side_effects=True),
        name="gather_features",
    )(own, other, targets)


def invert(m, width=8):
    side = m.shape[0]
    lane = lax.broadcasted_iota(jnp.int32, m.shape, 1)
    sub = lax.broadcasted_iota(jnp.int32, m.shape, 0)
    for k in range(0, side, width):
        columns = [jnp.broadcast_to(m[:, k + i:k + i + 1], m.shape) for i in range(width)]
        rows = [m[k + i:k + i + 1, :] for i in range(width)]
        for i in range(width):
            at = k + i
            column = columns[i]
            inverse = 1.0 / column[at:at + 1, :]
            row = jnp.where(lane[0:1] == at, 1.0, rows[i]) * inverse
            swept = jnp.where(sub == at, -1.0, column)
            for j in range(i + 1, width):
                to = k + j
                rows[j] = jnp.where(lane[0:1] == at, 0.0, rows[j]) - column[to:to + 1, :] * row
                columns[j] = jnp.where(sub == at, 0.0, columns[j]) - swept * (columns[j][at:at + 1, :] * inverse)
            m = jnp.where((lane == at) | (sub == at), 0.0, m) - swept * row
    return m


def solve_kernel(a_ref, out_ref, work):
    size = a_ref.shape[0]
    side = 128
    high = lax.Precision.HIGHEST
    diagonal = lax.broadcasted_iota(jnp.int32, a_ref.shape, 0) == lax.broadcasted_iota(jnp.int32, a_ref.shape, 1)
    work[...] = a_ref[...] + jnp.where(diagonal, DAMPING, 0.0)

    def body(block, carry):
        here = pl.ds(pl.multiple_of(block * side, side), side)
        rows = jnp.dot(invert(work[here, here]), work[here, :], precision=high, preferred_element_type=jnp.float32)
        work[...] = work[...] - jnp.dot(work[:, here], rows, precision=high, preferred_element_type=jnp.float32)
        work[here, :] = rows
        return carry

    lax.fori_loop(0, size // side, body, 0)
    out_ref[...] = lax.dot_general(
        jnp.ones((8, a_ref.shape[1] - size), jnp.float32),
        work[:, size:],
        (((1,), (1,)), ((), ())),
        precision=high,
        preferred_element_type=jnp.float32,
    )


def solve(extended):
    return pl.pallas_call(
        solve_kernel,
        out_shape=jax.ShapeDtypeStruct((8, extended.shape[0]), jnp.float32),
        in_specs=[pl.BlockSpec(memory_space=pltpu.VMEM)],
        out_specs=pl.BlockSpec(memory_space=pltpu.VMEM),
        scratch_shapes=[pltpu.VMEM(extended.shape, jnp.float32)],
        name="solve",
    )(extended)[0]


def block_kernel(
    x_ref, g_ref, other_x_ref, other_g_ref, w_ref, sketch_ref, sketch_in_ref, out_ref, hq_ref, dq_ref
):
    step = pl.program_id(0)
    length = x_ref.shape[1]

    @pl.when(step == 0)
    def _():
        hq_ref[...] = jnp.zeros_like(hq_ref)
        dq_ref[...] = jnp.zeros_like(dq_ref)

    pairs = [(x_ref, g_ref, 0), (x_ref, g_ref, 1), (other_x_ref, other_g_ref, 0), (other_x_ref, other_g_ref, 1)]
    sketch = sketch_ref[...]
    across = (((1,), (1,)), ((), ()))
    for n, (xs, gs, at) in enumerate(pairs):
        pre = lax.dot_general(xs[at], w_ref[0], across, preferred_element_type=jnp.float32)
        back = lax.dot_general(gs[at], w_ref[1], across, preferred_element_type=jnp.float32)
        sig = jax.nn.sigmoid(pre)
        hidden = (pre * sig).astype(jnp.bfloat16)
        slope = (back * sig * (1.0 + pre * (1.0 - sig))).astype(jnp.bfloat16)
        hq_ref[n] += jnp.dot(hidden, sketch, preferred_element_type=jnp.float32)
        dq_ref[n] += jnp.dot(slope, sketch, preferred_element_type=jnp.float32)

    @pl.when(step == pl.num_programs(0) - 1)
    def _():
        for n, (xs, gs, at) in enumerate(pairs):
            xp = jnp.dot(xs[at], sketch_in_ref[...], preferred_element_type=jnp.float32)
            gp = jnp.dot(gs[at], sketch_in_ref[...], preferred_element_type=jnp.float32)
            for which, (left, right) in enumerate([(dq_ref[n], xp), (hq_ref[n], gp)]):
                out_ref[n, which] = lax.dot_general(
                    left, right, (((0,), (0,)), ((), ())),
                    precision=lax.Precision.HIGHEST, preferred_element_type=jnp.float32,
                ) * (1.0 / length)


def partial_features(samples, cotangent, other_x, other_g, weights, sketch_rows, sketch_in):
    count, length, width = samples.shape
    hidden_units, rank = sketch_rows.shape
    chunk = 256
    whole = pl.BlockSpec((count, length, width), lambda i: (0, 0, 0))
    return pl.pallas_call(
        block_kernel,
        grid=(hidden_units // chunk,),
        out_shape=jax.ShapeDtypeStruct((2 * count, 2, rank, rank), jnp.float32),
        in_specs=[whole] * 4 + [
            pl.BlockSpec((2, chunk, width), lambda i: (0, i, 0)),
            pl.BlockSpec((chunk, rank), lambda i: (i, 0)),
            pl.BlockSpec((width, rank), lambda i: (0, 0)),
        ],
        out_specs=pl.BlockSpec((2 * count, 2, rank, rank), lambda i: (0, 0, 0, 0)),
        scratch_shapes=[
            pltpu.VMEM((2 * count, length, rank), jnp.float32),
            pltpu.VMEM((2 * count, length, rank), jnp.float32),
        ],
        compiler_params=pltpu.CompilerParams(vmem_limit_bytes=48 * 2**20),
        name="pointwise_block",
    )(samples, cotangent, other_x, other_g, weights, sketch_rows, sketch_in)


def per_device(samples, cotangent, w_in, w_out, sketch_in, sketch_hidden, targets):
    count, length, width = samples.shape
    rows = w_in.shape[0]
    weights, other_x, other_g = gather_weights(samples, cotangent, w_in, w_out)
    core = lax.axis_index("fsdp") % 2
    sketch_rows = lax.dynamic_index_in_dim(
        sketch_hidden.reshape(NZ * 2, 2, rows, -1), core, 1, keepdims=False
    ).reshape(NZ * 2 * rows, -1)
    partial = partial_features(
        samples, cotangent, other_x, other_g, weights.reshape(2, -1, width), sketch_rows, sketch_in
    ).reshape(2 * count, -1)
    own, other = partial[:count], partial[count:]
    table = gather_features(own, other, targets.reshape(count, 1))
    size = own.shape[1]
    table = table.reshape(-1, size + 128)
    everyone = table[:, :size]
    extended = lax.dot_general(
        everyone, table, (((0,), (0,)), ((), ())), preferred_element_type=jnp.float32
    )
    step = solve(extended)
    x, y, z, core = position()
    start = (core * 16 + x * 4 + y) * 32 + z * count
    feats = lax.dynamic_slice_in_dim(everyone, start, count, 0)
    fitted = jnp.dot(feats.astype(jnp.float32), step, precision=lax.Precision.HIGHEST)
    coeffs = (targets - fitted) / DAMPING
    return (coeffs, step)


def solution(mesh):
    in_specs = (
        P(("dp", "fsdp"), None, None),
        P(("dp", "fsdp"), None, None),
        P("fsdp", None),
        P("fsdp", None),
        P(),
        P(),
        P(("dp", "fsdp")),
    )
    out_specs = (P(("dp", "fsdp")), P())
    return jax.shard_map(
        per_device, mesh=mesh, in_specs=in_specs, out_specs=out_specs, check_vma=False
    )
```

```python
import jax
import jax.numpy as jnp
from jax import lax
from jax.experimental import pallas as pl
from jax.experimental.pallas import tpu as pltpu
from jax.sharding import PartitionSpec as P

DAMPING = 0.5
NZ, NY, NX = 16, 4, 4
MESH = pl.DeviceIdType.MESH


def position():
    group, member = lax.axis_index("dp"), lax.axis_index("fsdp")
    x = (group // 4) * 2 + (member // 2) % 2
    return x, group % 4, member // 4, member % 2


def device(x, y, z, core):
    return ((x // 2) * 4 + y, z * 4 + (x % 2) * 2 + core)


def greet(partners):
    barrier = pltpu.get_barrier_semaphore()
    for partner in partners:
        pl.semaphore_signal(barrier, inc=1, device_id=partner, device_id_type=MESH)
    pl.semaphore_wait(barrier, len(partners))


def weights_kernel(
    x_ref, g_ref, w_ref, all_ref, px_ref, pg_ref,
    swap_send, swap_recv, local_sem, z_send, z_recv, y_send, y_recv, o_send, o_recv, x_send, x_recv,
):
    x, y, z, core = position()
    low = x % 2
    up, down = (z + 1) % NZ, (z + NZ - 1) % NZ
    up2, down2 = (z + 2) % NZ, (z + NZ - 2) % NZ
    y_up, y_down = (y + 1) % NY, (y + NY - 1) % NY
    x_up, x_down = (x + 1) % NX, (x + NX - 1) % NX
    greet([
        device(x, y, up, core), device(x, y, down, core),
        device(x, y, up2, core), device(x, y, down2, core),
        device(x, y_up, z, core), device(x, y_down, z, core),
        device(x_up, y, z, core), device(x_down, y, z, core),
        device(x, y, z, 1 - core),
    ])
    sends = []

    def place(zz, q, lo):
        return all_ref.at[q // 2, zz, lo, q % 2]

    def remote(src, dst, send, recv, target):
        return pltpu.make_async_remote_copy(
            src_ref=src, dst_ref=dst, send_sem=send, recv_sem=recv, device_id=target, device_id_type=MESH
        )

    def start(copy):
        copy.start()
        sends.append(copy)

    def send_x(src, zz, q):
        target = device((x + (q // 2) * 2 + NX - 1) % NX, y, z, core)
        start(remote(src, place(zz, q, low), x_send.at[zz, q], x_recv.at[zz, q], target))

    def send_y(src, zz):
        start(remote(src, place(zz, y, low), y_send.at[0, zz], y_recv.at[0, zz], device(x, y_up, z, core)))
        start(remote(src, place(zz, y, low), y_send.at[1, zz], y_recv.at[1, zz], device(x, y_down, z, core)))

    def wait_recv(dst, recv):
        remote(dst, dst, swap_send.at[0], recv, device(x, y, z, 1 - core)).wait_recv()

    mine = w_ref.at[y // 2, y % 2]
    start(remote(mine, place(z, y, low), z_send.at[0, 1], z_recv.at[0, 1], device(x, y, up, core)))
    start(remote(mine, place(z, y, low), z_send.at[1, 1], z_recv.at[1, 1], device(x, y, down, core)))
    start(remote(mine, place(z, y, low), z_send.at[0, 2], z_recv.at[0, 2], device(x, y, up2, core)))
    start(remote(mine, place(z, y, low), z_send.at[1, 2], z_recv.at[1, 2], device(x, y, down2, core)))
    for q in range(4):
        send_x(w_ref.at[q // 2, q % 2], z, q)
    locals_ = []
    for q in range(4):
        copy = pltpu.make_async_copy(w_ref.at[q // 2, q % 2], place(z, q, low), local_sem.at[q])
        copy.start()
        locals_.append(copy)
    start(remote(x_ref, px_ref, swap_send.at[0], swap_recv.at[0], device(x, y, z, 1 - core)))
    start(remote(g_ref, pg_ref, swap_send.at[1], swap_recv.at[1], device(x, y, z, 1 - core)))

    def blocks_of(step):
        found = []
        if 1 <= step <= 8:
            found.append((0, (z + NZ - step) % NZ))
        if 1 <= step <= 7:
            found.append((1, (z + step) % NZ))
        return found

    for step in range(1, 11):
        for way, zz in blocks_of(step):
            here = place(zz, y, low)
            wait_recv(here, z_recv.at[way, step])
            if step + 2 <= (8 if way == 0 else 7):
                target = device(x, y, up2 if way == 0 else down2, core)
                start(remote(here, here, z_send.at[way, step + 2], z_recv.at[way, step + 2], target))
            send_y(here, zz)
            send_x(here, zz, y)
        for way, zz in blocks_of(step - 1):
            below, above = place(zz, y_down, low), place(zz, y_up, low)
            wait_recv(below, y_recv.at[0, zz])
            wait_recv(above, y_recv.at[1, zz])
            if way == 0:
                start(remote(below, below, o_send.at[zz], o_recv.at[zz], device(x, y_up, z, core)))
            else:
                start(remote(above, above, o_send.at[zz], o_recv.at[zz], device(x, y_down, z, core)))
            send_x(below, zz, y_down)
            send_x(above, zz, y_up)
        for way, zz in blocks_of(step - 2):
            far = (y + 2) % NY
            wait_recv(place(zz, far, low), o_recv.at[zz])
            send_x(place(zz, far, low), zz, far)
    for zz in range(NZ):
        for q in range(4):
            wait_recv(place(zz, q, 1 - low), x_recv.at[zz, q])
    wait_recv(px_ref, swap_recv.at[0])
    wait_recv(pg_ref, swap_recv.at[1])
    for copy in locals_:
        copy.wait()
    for copy in sends:
        copy.wait_send()


def gather_weights(flat_x, flat_g, w_in, w_out):
    rows, width = w_in.shape
    half = rows // 2
    w = jnp.stack([w_in, w_out]).reshape(2, 2, half, width)
    anywhere = pl.BlockSpec(memory_space=pl.ANY)
    sem = pltpu.SemaphoreType.DMA
    return pl.pallas_call(
        weights_kernel,
        out_shape=(
            jax.ShapeDtypeStruct((2, NZ, 2, 2, half, width), w.dtype),
            jax.ShapeDtypeStruct(flat_x.shape, flat_x.dtype),
            jax.ShapeDtypeStruct(flat_g.shape, flat_g.dtype),
        ),
        in_specs=[anywhere] * 3,
        out_specs=(anywhere,) * 3,
        scratch_shapes=[
            sem((2,)), sem((2,)), sem((4,)), sem((2, 9)), sem((2, 9)), sem((2, NZ)), sem((2, NZ)),
            sem((NZ,)), sem((NZ,)), sem((NZ, 4)), sem((NZ, 4)),
        ],
        compiler_params=pltpu.CompilerParams(collective_id=0, has_side_effects=True),
        name="gather_weights",
    )(flat_x, flat_g, w)


def features_kernel(
    own_ref, other_ref, targets_ref, f_ref, got, zbuf, wide,
    swap_send, swap_recv, z_send, z_recv, y_send, y_recv, x_send, x_recv, c_send, c_recv,
):
    x, y, z, core = position()
    along_z = [device(x, y, (z + d) % NZ, core) for d in range(1, NZ)]
    along_y = [device(x, (y + d) % NY, z, core) for d in range(1, 4)]
    along_x = [device((x + d) % NX, y, z, core) for d in range(1, 4)]
    partner = device(x, y, z, 1 - core)
    greet(along_z + along_y + along_x + [partner])

    def remote(src, dst, send, recv, target):
        return pltpu.make_async_remote_copy(
            src_ref=src, dst_ref=dst, send_sem=send, recv_sem=recv, device_id=target, device_id_type=MESH
        )

    def begin(mine, send, recv, partners):
        copies = []
        for d, target in enumerate(partners):
            copy = remote(mine, mine, send.at[d], recv.at[d], target)
            copy.start()
            copies.append(copy)
        return copies

    def finish(theirs, send, recv, partners):
        for d, target in enumerate(partners):
            remote(theirs[d], theirs[d], send.at[d], recv.at[d], target).wait_recv()

    swap = remote(other_ref, got, swap_send, swap_recv, partner)
    swap.start()
    swap.wait_recv()
    feats = own_ref[...] + got[...]
    t = targets_ref[...]
    high_t = t.astype(jnp.bfloat16).astype(jnp.float32)
    mid_t = (t - high_t).astype(jnp.bfloat16).astype(jnp.float32)
    low_t = t - high_t - mid_t
    lane = lax.broadcasted_iota(jnp.int32, (2, 128), 1)
    tail = jnp.where(lane == 0, high_t, jnp.where(lane == 1, mid_t, jnp.where(lane == 2, low_t, 0.0)))
    size = feats.shape[1]
    zbuf[z, :, 0:size] = feats.astype(jnp.bfloat16)
    zbuf[z, :, size:] = tail.astype(jnp.bfloat16)
    sends = [swap]
    sends += begin(zbuf.at[z], z_send, z_recv, along_z)
    finish([zbuf.at[(z + NZ - d) % NZ] for d in range(1, NZ)], z_send, z_recv, along_z)
    for zz in range(NZ):
        wide[2 * zz:2 * zz + 2, :] = zbuf[zz].astype(jnp.float32)
    packed = wide[...].astype(jnp.bfloat16)
    f_ref[core, x, y, 0] = packed[0:NZ]
    f_ref[core, x, y, 1] = packed[NZ:]
    ys = [(y + 4 - d) % NY for d in range(1, 4)]
    xs = [(x + 4 - d) % NX for d in range(1, 4)]
    sends += begin(f_ref.at[core, x, y, 0], y_send.at[0], y_recv.at[0], along_y)
    sends += begin(f_ref.at[core, x, y, 1], x_send.at[0], x_recv.at[0], along_x)
    finish([f_ref.at[core, x, yy, 0] for yy in ys], y_send.at[0], y_recv.at[0], along_y)
    sends += begin(f_ref.at[core, x, :, 0], x_send.at[1], x_recv.at[1], along_x)
    finish([f_ref.at[core, xx, y, 1] for xx in xs], x_send.at[0], x_recv.at[0], along_x)
    sends += begin(f_ref.at[core, :, y, 1], y_send.at[1], y_recv.at[1], along_y)
    finish([f_ref.at[core, xx, :, 0] for xx in xs], x_send.at[1], x_recv.at[1], along_x)
    finish([f_ref.at[core, :, yy, 1] for yy in ys], y_send.at[1], y_recv.at[1], along_y)
    sends += begin(f_ref.at[core], c_send, c_recv, [partner])
    finish([f_ref.at[1 - core]], c_send, c_recv, [partner])
    for copy in sends:
        copy.wait_send()


def gather_features(own, other, targets):
    size = own.shape[1]
    inside = pl.BlockSpec(memory_space=pltpu.VMEM)
    sem = pltpu.SemaphoreType.DMA
    return pl.pallas_call(
        features_kernel,
        out_shape=jax.ShapeDtypeStruct((2, NX, NY, 2, NZ, size + 128), jnp.bfloat16),
        in_specs=[inside] * 3,
        out_specs=inside,
        scratch_shapes=[
            pltpu.VMEM((2, size), jnp.float32),
            pltpu.VMEM((NZ, 2, size + 128), jnp.bfloat16),
            pltpu.VMEM((32, size + 128), jnp.float32),
            sem, sem, sem((NZ - 1,)), sem((NZ - 1,)), sem((2, 3)), sem((2, 3)), sem((2, 3)), sem((2, 3)),
            sem((1,)), sem((1,)),
        ],
        compiler_params=pltpu.CompilerParams(collective_id=1, has_side_effects=True),
        name="gather_features",
    )(own, other, targets)


def invert(m, width=8):
    side = m.shape[0]
    lane = lax.broadcasted_iota(jnp.int32, m.shape, 1)
    sub = lax.broadcasted_iota(jnp.int32, m.shape, 0)
    for k in range(0, side, width):
        columns = [jnp.broadcast_to(m[:, k + i:k + i + 1], m.shape) for i in range(width)]
        rows = [m[k + i:k + i + 1, :] for i in range(width)]
        for i in range(width):
            at = k + i
            column = columns[i]
            inverse = 1.0 / column[at:at + 1, :]
            row = jnp.where(lane[0:1] == at, 1.0, rows[i]) * inverse
            swept = jnp.where(sub == at, -1.0, column)
            for j in range(i + 1, width):
                to = k + j
                rows[j] = jnp.where(lane[0:1] == at, 0.0, rows[j]) - column[to:to + 1, :] * row
                columns[j] = jnp.where(sub == at, 0.0, columns[j]) - swept * (columns[j][at:at + 1, :] * inverse)
            m = jnp.where((lane == at) | (sub == at), 0.0, m) - swept * row
    return m


def solve_kernel(a_ref, out_ref, work):
    size = a_ref.shape[0]
    side = 128
    high = lax.Precision.HIGHEST
    diagonal = lax.broadcasted_iota(jnp.int32, a_ref.shape, 0) == lax.broadcasted_iota(jnp.int32, a_ref.shape, 1)
    work[...] = a_ref[...] + jnp.where(diagonal, DAMPING, 0.0)

    def body(block, carry):
        here = pl.ds(pl.multiple_of(block * side, side), side)
        rows = jnp.dot(invert(work[here, here]), work[here, :], precision=high, preferred_element_type=jnp.float32)
        work[...] = work[...] - jnp.dot(work[:, here], rows, precision=high, preferred_element_type=jnp.float32)
        work[here, :] = rows
        return carry

    lax.fori_loop(0, size // side, body, 0)
    out_ref[...] = lax.dot_general(
        jnp.ones((8, a_ref.shape[1] - size), jnp.float32),
        work[:, size:],
        (((1,), (1,)), ((), ())),
        precision=high,
        preferred_element_type=jnp.float32,
    )


def solve(extended):
    return pl.pallas_call(
        solve_kernel,
        out_shape=jax.ShapeDtypeStruct((8, extended.shape[0]), jnp.float32),
        in_specs=[pl.BlockSpec(memory_space=pltpu.VMEM)],
        out_specs=pl.BlockSpec(memory_space=pltpu.VMEM),
        scratch_shapes=[pltpu.VMEM(extended.shape, jnp.float32)],
        name="solve",
    )(extended)[0]


def block_kernel(
    x_ref, g_ref, other_x_ref, other_g_ref, w_ref, sketch_ref, sketch_in_ref, out_ref, hq_ref, dq_ref
):
    step = pl.program_id(0)
    length = x_ref.shape[1]

    @pl.when(step == 0)
    def _():
        hq_ref[...] = jnp.zeros_like(hq_ref)
        dq_ref[...] = jnp.zeros_like(dq_ref)

    pairs = [(x_ref, g_ref, 0), (x_ref, g_ref, 1), (other_x_ref, other_g_ref, 0), (other_x_ref, other_g_ref, 1)]
    sketch = sketch_ref[...]
    across = (((1,), (1,)), ((), ()))
    for n, (xs, gs, at) in enumerate(pairs):
        pre = lax.dot_general(xs[at], w_ref[0], across, preferred_element_type=jnp.float32)
        back = lax.dot_general(gs[at], w_ref[1], across, preferred_element_type=jnp.float32)
        sig = jax.nn.sigmoid(pre)
        hidden = (pre * sig).astype(jnp.bfloat16)
        slope = (back * sig * (1.0 + pre * (1.0 - sig))).astype(jnp.bfloat16)
        hq_ref[n] += jnp.dot(hidden, sketch, preferred_element_type=jnp.float32)
        dq_ref[n] += jnp.dot(slope, sketch, preferred_element_type=jnp.float32)

    @pl.when(step == pl.num_programs(0) - 1)
    def _():
        for n, (xs, gs, at) in enumerate(pairs):
            xp = jnp.dot(xs[at], sketch_in_ref[...], preferred_element_type=jnp.float32)
            gp = jnp.dot(gs[at], sketch_in_ref[...], preferred_element_type=jnp.float32)
            for which, (left, right) in enumerate([(dq_ref[n], xp), (hq_ref[n], gp)]):
                out_ref[n, which] = lax.dot_general(
                    left, right, (((0,), (0,)), ((), ())),
                    precision=lax.Precision.HIGHEST, preferred_element_type=jnp.float32,
                ) * (1.0 / length)


def partial_features(samples, cotangent, other_x, other_g, weights, sketch_rows, sketch_in):
    count, length, width = samples.shape
    hidden_units, rank = sketch_rows.shape
    chunk = 256
    whole = pl.BlockSpec((count, length, width), lambda i: (0, 0, 0))
    return pl.pallas_call(
        block_kernel,
        grid=(hidden_units // chunk,),
        out_shape=jax.ShapeDtypeStruct((2 * count, 2, rank, rank), jnp.float32),
        in_specs=[whole] * 4 + [
            pl.BlockSpec((2, chunk, width), lambda i: (0, i, 0)),
            pl.BlockSpec((chunk, rank), lambda i: (i, 0)),
            pl.BlockSpec((width, rank), lambda i: (0, 0)),
        ],
        out_specs=pl.BlockSpec((2 * count, 2, rank, rank), lambda i: (0, 0, 0, 0)),
        scratch_shapes=[
            pltpu.VMEM((2 * count, length, rank), jnp.float32),
            pltpu.VMEM((2 * count, length, rank), jnp.float32),
        ],
        compiler_params=pltpu.CompilerParams(vmem_limit_bytes=48 * 2**20),
        name="pointwise_block",
    )(samples, cotangent, other_x, other_g, weights, sketch_rows, sketch_in)


def per_device(samples, cotangent, w_in, w_out, sketch_in, sketch_hidden, targets):
    count, length, width = samples.shape
    rows = w_in.shape[0]
    weights, other_x, other_g = gather_weights(samples, cotangent, w_in, w_out)
    core = lax.axis_index("fsdp") % 2
    sketch_rows = lax.dynamic_index_in_dim(
        sketch_hidden.reshape(NZ * 2, 2, rows, -1), core, 1, keepdims=False
    ).reshape(NZ * 2 * rows, -1)
    partial = partial_features(
        samples, cotangent, other_x, other_g, weights.reshape(2, -1, width), sketch_rows, sketch_in
    ).reshape(2 * count, -1)
    own, other = partial[:count], partial[count:]
    table = gather_features(own, other, targets.reshape(count, 1))
    size = own.shape[1]
    table = table.reshape(-1, size + 128)
    everyone = table[:, :size]
    extended = lax.dot_general(
        everyone, table, (((0,), (0,)), ((), ())), preferred_element_type=jnp.float32
    )
    step = solve(extended)
    x, y, z, core = position()
    start = (core * 16 + x * 4 + y) * 32 + z * count
    feats = lax.dynamic_slice_in_dim(everyone, start, count, 0)
    fitted = jnp.dot(feats.astype(jnp.float32), step, precision=lax.Precision.HIGHEST)
    coeffs = (targets - fitted) / DAMPING
    return (coeffs, step)


def solution(mesh):
    in_specs = (
        P(("dp", "fsdp"), None, None),
        P(("dp", "fsdp"), None, None),
        P("fsdp", None),
        P("fsdp", None),
        P(),
        P(),
        P(("dp", "fsdp")),
    )
    out_specs = (P(("dp", "fsdp")), P())
    return jax.shard_map(
        per_device, mesh=mesh, in_specs=in_specs, out_specs=out_specs, check_vma=False
    )
```
